256 devices in a mesh: seg: 4 (over x), sec: 32 (over z, y), rep: 2 (over core).
Axes of the slice: x: 4, y: 4, z: 8, core: 2. Of those that a mesh axis runs over, the one named last changes fastest.
Arguments:
- psi: float32 [4, 64, 256, 256], P('seg', 'sec'), may hold values from -6 to 6
- left_env: bfloat16 [4, 18, 64, 256, 256], P('seg', 'rep', 'sec'), may hold values from -0.375 to 0.375
- right_env: bfloat16 [4, 18, 64, 256, 256], P('seg', 'rep', 'sec'), may hold values from -0.375 to 0.375
- local_block: bfloat16 [4, 64, 256, 256], P('seg', 'sec'), may hold values from -0.375 to 0.375
- kept_left: int32 [4, 64], P('seg', 'sec'), may hold values from 64 to 256
- kept_right: int32 [4, 64], P('seg', 'sec'), may hold values from 64 to 256
- pattern: int32 [4, 18, 64], P('seg', 'rep', 'sec'), may hold values 0 or 1
- term_charge: int32 [18], replicated, may hold values from -2 to 2
Outputs:
- last_vector: float32 [4, 64, 256, 256], P('seg', 'sec')
- coefficients: float32 [4, 8], P('seg')
The draws below stay inside these ranges and needn't reach their ends.
All inputs are finite; a program needn't handle non-finite values. No bound on the sum of `pattern` on one device may be relied on, other than what follows from the above.
Results may differ from the reference program's by a relative error of at most 0.012.
Values may be sent and summed in bfloat16 or wider, within the bound.
A program may use at most 64 MiB of HBM per device.

```python
import jax
import jax.numpy as jnp
from jax import lax

B = 256
W = 18
ITERS = 4
S = 64
NSEG = 4


def place_ends(drawn, stream_key, least, high):
    longest = drawn.shape.index(max(drawn.shape))
    spots = []
    for shift in (0, 1):
        where = [jax.random.randint(jax.random.fold_in(stream_key, axis), (), 0, length) for axis, length in enumerate(drawn.shape)]
        where[longest] = (where[longest] + shift) % drawn.shape[longest]
        spots.append(tuple(where))
    return drawn.at[spots[0]].set(least).at[spots[1]].set(high)


def block_scale(own_key, shape, shards, smallest, top_value):
    def one(dim, parts):
        heights = jax.random.uniform(jax.random.fold_in(jax.random.fold_in(own_key, 6), dim), (parts,), jnp.float32, smallest / len(shards), top_value / len(shards))
        return jnp.repeat(jnp.exp(heights), shape[dim] // parts).reshape((-1,) + (1,) * (len(shape) - dim - 1))

    level = one(*shards[0])
    for cut in shards[1:]:
        level = level * one(*cut)
    return level


def centred(rng, dims, deviation, bound, pieces=(), held_as=jnp.bfloat16):
    entries = jax.random.normal(rng, dims, jnp.float32) * deviation
    if len(pieces) > 0:
        entries = block_scale(rng, dims, pieces, -0.22, 0.18) * entries
    return jnp.clip(entries, min=-bound, max=bound).astype(held_as)


def setup_inputs(seed: int = 0) -> dict:
    key_list = jax.random.split(jax.random.key(seed), 9)
    psi = centred(key_list[0], (NSEG, S, B, B), 1.0, 6.0, ((0, 4), (1, 32)), jnp.float32)
    left_env = centred(key_list[1], (NSEG, W, S, B, B), B ** -0.5, 0.375, ((0, 4), (1, 2), (2, 32)))
    right_env = centred(key_list[2], (NSEG, W, S, B, B), B ** -0.5, 0.375, ((0, 4), (1, 2), (2, 32)))
    local_block = centred(key_list[3], (NSEG, S, B, B), B ** -0.5, 0.375, ((0, 4), (1, 32)))
    kept_left = place_ends(jax.random.randint(key_list[4], (NSEG, S), B // 4, B + 1), jax.random.fold_in(key_list[4], 1), B // 4, B).astype(jnp.int32)
    kept_right = place_ends(jax.random.randint(key_list[5], (NSEG, S), B // 4, B + 1), jax.random.fold_in(key_list[5], 1), B // 4, B).astype(jnp.int32)
    pattern = place_ends((jax.random.randint(key_list[6], (NSEG, W, S), 0, 4) < 3).astype(jnp.int32), jax.random.fold_in(key_list[6], 1), 0, 1)
    term_charge = place_ends(jax.random.randint(key_list[7], (W,), -2, 3), jax.random.fold_in(key_list[7], 1), -2, 2).astype(jnp.int32)
    return {"psi": psi, "left_env": left_env, "right_env": right_env, "local_block": local_block, "kept_left": kept_left, "kept_right": kept_right, "pattern": pattern, "term_charge": term_charge}


def one_segment(items, charges):
    start, lefts, rights, block, keep_l, keep_r, pat = items
    states = lax.iota(jnp.int32, B)
    rows = (states[None, :] < keep_l[:, None]).astype(jnp.float32)
    cols = (states[None, :] < keep_r[:, None]).astype(jnp.float32)
    projector = rows[:, :, None] * cols[:, None, :]
    left_f = lefts.astype(jnp.float32)
    right_f = rights.astype(jnp.float32)
    block_f = block.astype(jnp.float32)
    pat_f = pat.astype(jnp.float32)
    index = (lax.iota(jnp.int32, S)[None, :] + 2 + charges[:, None]).astype(jnp.int32)

    def apply_op(vector):
        vb = vector.astype(jnp.bfloat16).astype(jnp.float32)
        padded = jnp.pad(vb, ((2, 2), (0, 0), (0, 0)))
        moved = padded[index]
        inner = jnp.einsum('wsij,wsjk->wsik', left_f, moved)
        inner = (inner * pat_f[:, :, None, None]).astype(jnp.bfloat16).astype(jnp.float32)
        total = jnp.einsum('wsik,wslk->sil', inner, right_f)
        local = jnp.einsum('sij,sjk->sik', block_f, vb) + jnp.einsum('sij,skj->sik', vb, block_f)
        return projector * (total + local)
    first = projector * start
    vector = first / jnp.sqrt(jnp.mean(first * first) + 1e-06)
    prev = jnp.zeros_like(vector)
    beta_prev = jnp.float32(0.0)
    alphas = []
    betas = []
    for step in range(ITERS):
        image = apply_op(vector)
        alpha = jnp.mean(vector * image)
        image = image - alpha * vector - beta_prev * prev
        beta = jnp.sqrt(jnp.mean(image * image) + 1e-06)
        prev = vector
        vector = image / beta
        beta_prev = beta
        alphas.append(alpha)
        betas.append(beta)
    return (vector, jnp.stack(alphas + betas))

def reference(psi, left_env, right_env, local_block, kept_left, kept_right, pattern, term_charge):
    lefts = jnp.roll(left_env, 1, axis=0)
    rights = jnp.roll(right_env, -1, axis=0)
    charges = term_charge.astype(jnp.int32)
    last_vector, coefficients = lax.map(lambda items: one_segment(items, charges), (psi, lefts, rights, local_block, kept_left, kept_right, pattern))
    return (last_vector, coefficients)
```

```python
import functools

import jax
import jax.numpy as jnp
from jax import lax
from jax.experimental import pallas as pl
from jax.experimental.pallas import tpu as pltpu
from jax.sharding import PartitionSpec as P

ITERS = 4
NY = 4
HALO = 2
F32 = jnp.float32
BF16 = jnp.bfloat16
MESH = pl.DeviceIdType.MESH


def nt_dot(a, b):
    return lax.dot_general(a, b, (((1,), (1,)), ((), ())), preferred_element_type=F32)


def column_sums(x):
    total = jnp.sum(x, axis=0, keepdims=True)
    width = total.shape[1] // 2
    return total[:, :width] + total[:, width:]


def kernel(
    nseg, nsec, here, size, count,
    psi, left, right, block, keep_l, keep_r, pattern, charge,
    out, coeffs,
    lbuf, rbuf, vs0, vs1, vs2, vs3, acc, mask, vs, us, ws, theirs,
    pat, index, red_z, red_y,
    l_send, r_send, l_recv, r_recv, halo_send, halo_recv,
    z_send, z_recv, y_send, y_recv, pat_send, pat_recv, fin_send, fin_recv,
):
    slots = (vs0, vs1, vs2, vs3)
    seg, sec, rep = lax.axis_index("seg"), lax.axis_index("sec"), lax.axis_index("rep")
    nz = nsec // NY
    z, y = sec // NY, sec % NY
    other = 1 - rep
    sector, sectors = 2 * sec + rep, 2 * nsec
    ahead, behind = (seg + 1) % nseg, (seg + nseg - 1) % nseg
    terms = 2 * here

    def at_sector(shift):
        s = (sector + sectors + shift) % sectors
        return (seg, s // 2, s % 2)

    shifts = (-1, 1, -2, 2)
    z_peers = [(seg, ((z + i) % nz) * NY + y, rep) for i in range(1, nz)]
    mine_y = 2 * y + rep
    y_peers = []
    for i in range(1, 2 * NY):
        p = (mine_y + i) % (2 * NY)
        y_peers.append((seg, z * NY + p // 2, p % 2))

    partners = [(a, sec, jnp.int32(r)) for a in (ahead, behind) for r in range(2)]
    partners += [at_sector(d) for d in shifts] + z_peers + y_peers
    barrier = pltpu.get_barrier_semaphore()
    for p in partners:
        pl.semaphore_signal(barrier, inc=1, device_id=p, device_id_type=MESH)
    pl.semaphore_wait(barrier, len(partners))

    def left_copy(t, r):
        w = rep * here + t
        return pltpu.make_async_remote_copy(
            left.at[0, t, r], lbuf.at[w], l_send, l_recv.at[w],
            device_id=(ahead, sec, jnp.int32(r)), device_id_type=MESH,
        )

    def right_copy(t, r):
        w = rep * here + t
        return pltpu.make_async_remote_copy(
            right.at[0, t, r], rbuf.at[w], r_send, r_recv.at[w],
            device_id=(behind, sec, jnp.int32(r)), device_id_type=MESH,
        )

    @pl.loop(0, here)
    def _(t):
        for r in range(2):
            left_copy(t, r).start()
            right_copy(t, r).start()

    def start_halo(k):
        for n, d in enumerate(shifts):
            pltpu.make_async_remote_copy(
                slots[k].at[HALO], slots[k].at[HALO - d],
                halo_send.at[k, n], halo_recv.at[k, n],
                device_id=at_sector(d), device_id_type=MESH,
            ).start()

    def wait_halo(k):
        for n, d in enumerate(shifts):
            pltpu.make_async_remote_copy(
                slots[k].at[HALO], slots[k].at[HALO - d],
                halo_send.at[k, n], halo_recv.at[k, n],
                device_id=at_sector(d), device_id_type=MESH,
            ).wait_recv()

    def exchange_start(buf, k, mine, peers, send, recv):
        for p in peers:
            pltpu.make_async_remote_copy(
                buf.at[k, mine], buf.at[k, mine], send.at[k], recv.at[k],
                device_id=p, device_id_type=MESH,
            ).start()

    def exchange_wait(buf, k, n, sem):
        some = buf.at[k, pl.ds(0, n)]
        pltpu.make_async_copy(some, some, sem.at[k]).wait()

    def total_of(buf, k, n):
        total = buf[k, 0]
        for i in range(1, n):
            total = total + buf[k, i]
        return total

    def reduce_first(k, rows):
        red_z[k, z] = jnp.zeros_like(red_z[k, 0])
        for i, row in enumerate(rows):
            red_z[k, z, pl.ds(i, 1), :] = row
        exchange_start(red_z, k, z, z_peers, z_send, z_recv)

    def reduce_second(k):
        exchange_wait(red_z, k, nz - 1, z_recv)
        red_y[k, mine_y] = total_of(red_z, k, nz)
        exchange_start(red_y, k, mine_y, y_peers, y_send, y_recv)

    def reduce_last(k):
        exchange_wait(red_y, k, 2 * NY - 1, y_recv)
        total = jnp.sum(total_of(red_y, k, 2 * NY), axis=1, keepdims=True)
        return total * (1.0 / count)

    rows = lax.broadcasted_iota(jnp.int32, (size, size), 0)
    cols = lax.broadcasted_iota(jnp.int32, (size, size), 1)
    inside = (rows < keep_l[0, rep]) & (cols < keep_r[0, rep])
    mask[...] = inside.astype(F32)
    start = mask[...] * psi[0, rep]
    vs[0] = start
    reduce_first(ITERS, [column_sums(start * start)])

    both = pattern[0].astype(F32)
    wide = (here, pat.shape[2])
    first, second = (jnp.broadcast_to(both[:, i : i + 1], wide) for i in range(2))
    zero = rep == 0
    pat[rep, pl.ds(0, here), :] = jnp.where(zero, first, second)
    pat[2, pl.ds(0, here), :] = jnp.where(zero, second, first)
    pat_copy = pltpu.make_async_remote_copy(
        pat.at[2], pat.at[rep], pat_send, pat_recv,
        device_id=(seg, sec, other), device_id_type=MESH,
    )
    pat_copy.start()
    pat_back = pltpu.make_async_remote_copy(
        pat.at[2], pat.at[other], pat_send, pat_recv,
        device_id=(seg, sec, other), device_id_type=MESH,
    )

    for k in range(ITERS):
        slots[k][2 * HALO + 1] = jnp.zeros((size, size), BF16)

    @pl.loop(0, terms)
    def _(w):
        c = charge[w]
        to = sector + c
        index[w] = jnp.where((to >= 0) & (to < sectors), c + HALO, 2 * HALO + 1)

    reduce_second(ITERS)
    scale = reduce_last(ITERS)[0:1]
    v0 = vs[0] * lax.rsqrt(scale + 1e-06)
    vs[0] = v0
    slots[0][HALO] = v0.astype(BF16)
    start_halo(0)
    pat_back.wait_recv()

    def local(k):
        own, blk = slots[k][HALO], block[0, rep]
        return jnp.dot(blk, own, preferred_element_type=F32) + nt_dot(own, blk)

    def term(k, q, t):
        w = q * here + t
        moved = slots[k][index[w]]
        inner = jnp.dot(lbuf[w], moved, preferred_element_type=F32)
        row = pat[q, pl.ds(t, 1), :]
        inner = (inner * jnp.concatenate([row, row], axis=1)).astype(BF16)
        return nt_dot(inner, rbuf[w])

    def env_wait(w):
        pltpu.make_async_remote_copy(
            left.at[0, 0, 0], lbuf.at[w], l_send, l_recv.at[w],
            device_id=(ahead, sec, rep), device_id_type=MESH,
        ).wait_recv()
        pltpu.make_async_remote_copy(
            right.at[0, 0, 0], rbuf.at[w], r_send, r_recv.at[w],
            device_id=(behind, sec, rep), device_id_type=MESH,
        ).wait_recv()

    acc[...] = local(0)
    wait_halo(0)

    @pl.loop(0, here)
    def _(t):
        env_wait(t)
        env_wait(here + t)
        acc[...] += term(0, 0, t) + term(0, 1, t)

    alphas, betas = [], []
    for k in range(ITERS):
        hv = mask[...] * acc[...]
        if k == 0:
            us[0] = hv
            ws[0] = hv
        else:
            means = reduce_last(k - 1)
            alpha = means[0:1]
            rest = means[1:2] - 2.0 * alpha * means[2:3] + alpha * alpha * means[3:4]
            beta = jnp.sqrt(jnp.maximum(rest, 0.0) + 1e-06)
            alphas.append(alpha)
            betas.append(beta)
            inverse = 1.0 / beta
            u = (hv - alpha * us[k - 1]) * inverse
            us[k] = u
            ws[k] = u - beta * vs[k - 1]
        if k < ITERS - 1:
            slots[k + 1][HALO] = ws[k].astype(BF16)
            start_halo(k + 1)
        if k > 0:
            vs[k] = (ws[k - 1] - alpha * vs[k - 1]) * inverse
        v, u, w = vs[k], us[k], ws[k]
        reduce_first(k, [column_sums(v * u), column_sums(w * w), column_sums(v * w), column_sums(v * v)])
        if k < ITERS - 1:
            acc[...] = local(k + 1)
            reduce_second(k)
            wait_halo(k + 1)

            @pl.loop(0, here)
            def _(t):
                acc[...] += term(k + 1, 0, t) + term(k + 1, 1, t)

    last = ITERS - 1

    def final_copy(i, buf):
        return pltpu.make_async_remote_copy(
            buf.at[last], theirs.at[i], fin_send.at[i], fin_recv.at[i],
            device_id=(seg, sec, other), device_id_type=MESH,
        )

    final_copy(0, ws).start()
    final_copy(1, vs).start()
    reduce_second(last)
    means = reduce_last(last)
    alpha = means[0:1]
    rest = means[1:2] - 2.0 * alpha * means[2:3] + alpha * alpha * means[3:4]
    beta = jnp.sqrt(jnp.maximum(rest, 0.0) + 1e-06)
    inverse = 1.0 / beta
    coeffs[...] = jnp.concatenate(alphas + [alpha] + betas + [beta], axis=1)
    out[0, rep] = (ws[last] - alpha * vs[last]) * inverse
    final_copy(0, ws).wait_recv()
    final_copy(1, vs).wait_recv()
    out[0, other] = (theirs[0] - alpha * theirs[1]) * inverse

    pltpu.make_async_copy(left, left, l_send).wait()
    pltpu.make_async_copy(right, right, r_send).wait()
    pat_copy.wait_send()
    final_copy(0, ws).wait_send()
    final_copy(1, vs).wait_send()
    for k in range(ITERS):
        for n, d in enumerate(shifts):
            pltpu.make_async_remote_copy(
                slots[k].at[HALO], slots[k].at[HALO - d],
                halo_send.at[k, n], halo_recv.at[k, n],
                device_id=at_sector(d), device_id_type=MESH,
            ).wait_send()
    for k in range(ITERS + 1):
        exchange_wait(red_z, k, nz - 1, z_send)
        exchange_wait(red_y, k, 2 * NY - 1, y_send)


def on_device(nseg, nsec, psi, left, right, block, keep_l, keep_r, pattern, charge):
    here, size = left.shape[1], left.shape[3]
    count = 2 * nsec * size * size
    nz = nsec // NY
    vmem = pl.BlockSpec(memory_space=pltpu.VMEM)
    smem = pl.BlockSpec(memory_space=pltpu.SMEM)
    anywhere = pl.BlockSpec(memory_space=pl.ANY)
    square = (size, size)
    dma = pltpu.SemaphoreType.DMA
    halo = pltpu.VMEM((2 * HALO + 2, *square), BF16)
    terms = 2 * here
    return pl.pallas_call(
        functools.partial(kernel, nseg, nsec, here, size, count),
        out_shape=(
            jax.ShapeDtypeStruct(psi.shape, F32),
            jax.ShapeDtypeStruct((1, 2 * ITERS), F32),
        ),
        in_specs=[vmem, anywhere, anywhere, vmem, smem, smem, vmem, smem],
        out_specs=(vmem, vmem),
        scratch_shapes=[
            pltpu.VMEM((terms, *square), BF16),
            pltpu.VMEM((terms, *square), BF16),
            halo, halo, halo, halo,
            pltpu.VMEM(square, F32),
            pltpu.VMEM(square, F32),
            pltpu.VMEM((ITERS, *square), F32),
            pltpu.VMEM((ITERS, *square), F32),
            pltpu.VMEM((ITERS, *square), F32),
            pltpu.VMEM((2, *square), F32),
            pltpu.VMEM((3, 16, 128), F32),
            pltpu.SMEM((terms,), jnp.int32),
            pltpu.VMEM((ITERS + 1, nz, 8, 128), F32),
            pltpu.VMEM((ITERS + 1, 2 * NY, 8, 128), F32),
            dma, dma, dma((terms,)), dma((terms,)),
            dma((ITERS, 4)), dma((ITERS, 4)),
            dma((ITERS + 1,)), dma((ITERS + 1,)),
            dma((ITERS + 1,)), dma((ITERS + 1,)),
            dma, dma, dma((2,)), dma((2,)),
        ],
        compiler_params=pltpu.CompilerParams(
            collective_id=0, has_side_effects=True, vmem_limit_bytes=48 << 20
        ),
    )(psi, left, right, block, keep_l, keep_r, pattern, charge)


def solution(mesh):
    placed = (
        P("seg", "sec", None, None),
        P("seg", "rep", "sec", None, None),
        P("seg", "rep", "sec", None, None),
        P("seg", "sec", None, None),
        P("seg", "sec"),
        P("seg", "sec"),
        P("seg", "rep", "sec"),
        P(),
    )
    return jax.shard_map(
        functools.partial(on_device, mesh.shape["seg"], mesh.shape["sec"]),
        mesh=mesh,
        in_specs=placed,
        out_specs=(P("seg", "sec", None, None), P("seg", None)),
        check_vma=False,
    )
```

```python
import functools

import jax
import jax.numpy as jnp
from jax import lax
from jax.experimental import pallas as pl
from jax.experimental.pallas import tpu as pltpu
from jax.sharding import PartitionSpec as P

ITERS = 4
NY = 4
HALO = 2
ROUNDS = 4
INITIAL = ROUNDS - 1
SUMS = 16
F32 = jnp.float32
BF16 = jnp.bfloat16
MESH = pl.DeviceIdType.MESH


def nt_dot(a, b):
    return lax.dot_general(a, b, (((1,), (1,)), ((), ())), preferred_element_type=F32)


def outward(n):
    return sorted(range(1, n), key=lambda i: -min(i, n - i))


def column_sums(x):
    total = jnp.sum(x, axis=0, keepdims=True)
    width = total.shape[1] // 2
    return total[:, :width] + total[:, width:]


def kernel(
    nseg, nsec, here, size, count,
    psi, left, right, block, keep_l, keep_r, pattern, charge,
    out, coeffs,
    lbuf, rbuf, vs0, vs1, vs2, vs3, acc, mask, v0, e1, e2, v1, u1, w1, hu1, hw1, mine, theirs,
    psi_v, blk_v, pat_v, pat_s, kl_s, kr_s, charge_s, index, red_z, red_y,
    load, l_send, r_send, l_recv, r_recv, halo_send, halo_recv,
    z_send, z_recv, y_send, y_recv, pat_send, pat_recv, fin_send, fin_recv,
):
    slots = (vs0, vs1, vs2, vs3)
    seg, sec, rep = lax.axis_index("seg"), lax.axis_index("sec"), lax.axis_index("rep")
    nz = nsec // NY
    z, y = sec // NY, sec % NY
    other = 1 - rep
    sector, sectors = 2 * sec + rep, 2 * nsec
    ahead, behind = (seg + 1) % nseg, (seg + nseg - 1) % nseg
    terms = 2 * here

    def at_sector(shift):
        s = (sector + sectors + shift) % sectors
        return (seg, s // 2, s % 2)

    shifts = (-1, 1, -2, 2)
    z_peers = [(seg, ((z + i) % nz) * NY + y, rep) for i in outward(nz)]
    mine_y = 2 * y + rep
    y_peers = []
    for i in outward(2 * NY):
        p = (mine_y + i) % (2 * NY)
        y_peers.append((seg, z * NY + p // 2, p % 2))

    partners = [(a, sec, jnp.int32(r)) for a in (ahead, behind) for r in range(2)]
    partners += [at_sector(d) for d in shifts] + z_peers + y_peers
    barrier = pltpu.get_barrier_semaphore()
    for p in partners:
        pl.semaphore_signal(barrier, inc=1, device_id=p, device_id_type=MESH)
    loads = [
        pltpu.make_async_copy(a, b, load.at[i])
        for i, (a, b) in enumerate([
            (psi.at[0, rep], psi_v), (block.at[0, rep], blk_v), (pattern.at[0], pat_s.at[rep]),
            (keep_l, kl_s), (keep_r, kr_s), (charge, charge_s),
        ])
    ]
    for c in loads:
        c.start()
    pl.semaphore_wait(barrier, len(partners))

    def left_copy(t, r):
        w = rep * here + t
        return pltpu.make_async_remote_copy(
            left.at[0, t, r], lbuf.at[w], l_send, l_recv.at[w],
            device_id=(ahead, sec, jnp.int32(r)), device_id_type=MESH,
        )

    def right_copy(t, r):
        w = rep * here + t
        return pltpu.make_async_remote_copy(
            right.at[0, t, r], rbuf.at[w], r_send, r_recv.at[w],
            device_id=(behind, sec, jnp.int32(r)), device_id_type=MESH,
        )

    @pl.loop(0, here)
    def _(t):
        for r in range(2):
            left_copy(t, r).start()
            right_copy(t, r).start()

    def start_halo(k):
        for n, d in enumerate(shifts):
            pltpu.make_async_remote_copy(
                slots[k].at[HALO], slots[k].at[HALO - d],
                halo_send.at[k, n], halo_recv.at[k, n],
                device_id=at_sector(d), device_id_type=MESH,
            ).start()

    def wait_halo(k):
        for n, d in enumerate(shifts):
            pltpu.make_async_remote_copy(
                slots[k].at[HALO], slots[k].at[HALO - d],
                halo_send.at[k, n], halo_recv.at[k, n],
                device_id=at_sector(d), device_id_type=MESH,
            ).wait_recv()

    def exchange_start(buf, k, mine, peers, send, recv):
        for p in peers:
            pltpu.make_async_remote_copy(
                buf.at[k, mine], buf.at[k, mine], send.at[k], recv.at[k],
                device_id=p, device_id_type=MESH,
            ).start()

    def exchange_wait(buf, k, n, sem):
        some = buf.at[k, pl.ds(0, n)]
        pltpu.make_async_copy(some, some, sem.at[k]).wait()

    def total_of(buf, k, n):
        total = buf[k, 0]
        for i in range(1, n):
            total = total + buf[k, i]
        return total

    def reduce_first(k, rows):
        red_z[k, z] = jnp.zeros_like(red_z[k, 0])
        for i, row in enumerate(rows):
            red_z[k, z, pl.ds(i, 1), :] = row
        exchange_start(red_z, k, z, z_peers, z_send, z_recv)

    def reduce_second(k):
        exchange_wait(red_z, k, nz - 1, z_recv)
        red_y[k, mine_y] = total_of(red_z, k, nz)
        exchange_start(red_y, k, mine_y, y_peers, y_send, y_recv)

    def reduce_last(k):
        exchange_wait(red_y, k, 2 * NY - 1, y_recv)
        total = jnp.sum(total_of(red_y, k, 2 * NY), axis=1, keepdims=True)
        return total * (1.0 / count)

    pat_copy = pltpu.make_async_remote_copy(
        pattern.at[0], pat_v, pat_send, pat_recv, device_id=(seg, sec, other), device_id_type=MESH
    )
    pat_copy.start()
    for c in loads:
        c.wait()

    rows = lax.broadcasted_iota(jnp.int32, (size, size), 0)
    cols = lax.broadcasted_iota(jnp.int32, (size, size), 1)
    inside = (rows < kl_s[0, rep]) & (cols < kr_s[0, rep])
    mask[...] = inside.astype(F32)
    start = mask[...] * psi_v[...]
    v0[...] = start
    reduce_first(INITIAL, [column_sums(start * start)])

    pat_copy.wait_recv()
    move = pltpu.make_async_copy(pat_v, pat_s.at[other], load.at[0])
    move.start()
    move.wait()

    for k in range(ITERS):
        slots[k][2 * HALO + 1] = jnp.zeros((size, size), BF16)

    @pl.loop(0, terms)
    def _(w):
        c = charge_s[w]
        to = sector + c
        index[w] = jnp.where((to >= 0) & (to < sectors), c + HALO, 2 * HALO + 1)

    reduce_second(INITIAL)
    scale = reduce_last(INITIAL)[0:1]
    v0[...] = v0[...] * lax.rsqrt(scale + 1e-06)
    slots[0][HALO] = v0[...].astype(BF16)
    start_halo(0)

    def apply_local(k):
        half = size // 2

        @pl.loop(0, 2)
        def _(i):
            some = pl.ds(pl.multiple_of(i * half, half), half)
            first = jnp.dot(blk_v[some, :], slots[k][HALO], preferred_element_type=F32)
            acc[some, :] = first + nt_dot(slots[k][HALO, some, :], blk_v[...])

    def term(k, q, t):
        w = q * here + t
        moved = slots[k][index[w]]
        inner = jnp.dot(lbuf[w], moved, preferred_element_type=F32)
        inner = (inner * pat_s[q, rep, t].astype(F32)).astype(BF16)
        return nt_dot(inner, rbuf[w])

    def env_wait(w):
        pltpu.make_async_remote_copy(
            left.at[0, 0, 0], lbuf.at[w], l_send, l_recv.at[w],
            device_id=(ahead, sec, rep), device_id_type=MESH,
        ).wait_recv()
        pltpu.make_async_remote_copy(
            right.at[0, 0, 0], rbuf.at[w], r_send, r_recv.at[w],
            device_id=(behind, sec, rep), device_id_type=MESH,
        ).wait_recv()

    def apply_rest(k):
        wait_halo(k)

        @pl.loop(0, here)
        def _(t):
            acc[...] += term(k, 0, t) + term(k, 1, t)

    def offer(k, x):
        slots[k][HALO] = x.astype(BF16)
        start_halo(k)

    def dot(a, b):
        return column_sums(a * b)

    def coefficients(means, vu, vw, vv, ww):
        alpha = means[vu : vu + 1]
        rest = means[ww : ww + 1] - 2.0 * alpha * means[vw : vw + 1] + alpha * alpha * means[vv : vv + 1]
        return alpha, jnp.sqrt(jnp.maximum(rest, 0.0) + 1e-06)

    apply_local(0)
    wait_halo(0)

    @pl.loop(0, here)
    def _(t):
        env_wait(t)
        env_wait(here + t)
        acc[...] += term(0, 0, t) + term(0, 1, t)

    e1[...] = mask[...] * acc[...]
    offer(1, e1[...])
    reduce_first(0, [dot(v0[...], e1[...]), dot(e1[...], e1[...]), dot(v0[...], v0[...])])
    apply_local(1)
    reduce_second(0)
    apply_rest(1)

    e2[...] = mask[...] * acc[...]
    offer(2, e2[...])
    alpha0, beta0 = coefficients(reduce_last(0), 0, 0, 2, 1)
    inverse0 = 1.0 / beta0
    v1[...] = (e1[...] - alpha0 * v0[...]) * inverse0
    u1[...] = (e2[...] - alpha0 * e1[...]) * inverse0
    w1[...] = u1[...] - beta0 * v0[...]
    reduce_first(1, [dot(v1[...], u1[...]), dot(v1[...], w1[...]), dot(v1[...], v1[...]), dot(w1[...], w1[...])])
    apply_local(2)
    reduce_second(1)
    apply_rest(2)

    hu1[...] = (mask[...] * acc[...] - alpha0 * e2[...]) * inverse0
    hw1[...] = hu1[...] - beta0 * e1[...]
    offer(3, hw1[...])
    apply_local(3)
    alpha1, beta1 = coefficients(reduce_last(1), 0, 1, 2, 3)
    inverse1 = 1.0 / beta1
    mine[0] = (w1[...] - alpha1 * v1[...]) * inverse1
    mine[1] = (hw1[...] - alpha1 * u1[...]) * inverse1
    mine[2] = mine[1] - beta1 * v1[...]

    def final_copy(i):
        return pltpu.make_async_remote_copy(
            mine.at[i], theirs.at[i], fin_send.at[i], fin_recv.at[i],
            device_id=(seg, sec, other), device_id_type=MESH,
        )

    for i in range(3):
        final_copy(i).start()
    hu1[...] = alpha1 * hu1[...] + beta1 * beta1 * u1[...]
    v2, u2, w2 = mine[0], mine[1], mine[2]
    early = [dot(v2, u2), dot(v2, w2), dot(v2, v2), dot(w2, w2), dot(w2, u2), dot(u2, u2)]
    apply_rest(3)

    mine[3] = (mask[...] * acc[...] - hu1[...]) * inverse1
    h, v2, u2, w2 = mine[3], mine[0], mine[1], mine[2]
    reduce_first(2, early + [dot(w2, h), dot(v2, h), dot(h, h), dot(u2, h)])
    final_copy(3).start()
    reduce_second(2)
    means = reduce_last(2)
    vu, vw, vv, ww, wu, uu, wh, vh, hh, uh = (means[i : i + 1] for i in range(10))
    alpha2, beta2 = coefficients(means, 0, 1, 2, 3)
    square2 = beta2 * beta2
    inverse2 = 1.0 / square2
    alpha3 = (wh - alpha2 * (wu + vh) + alpha2 * alpha2 * vu) * inverse2
    ww3 = (
        hh + alpha2 * alpha2 * uu + square2 * square2 * vv
        - 2.0 * (alpha2 * uh + square2 * vh) + 2.0 * alpha2 * square2 * vu
    ) * inverse2
    vv3 = (ww - 2.0 * alpha2 * vw + alpha2 * alpha2 * vv) * inverse2
    vw3 = alpha3 - vw + alpha2 * vv
    rest = ww3 - 2.0 * alpha3 * vw3 + alpha3 * alpha3 * vv3
    beta3 = jnp.sqrt(jnp.maximum(rest, 0.0) + 1e-06)
    coeffs[...] = jnp.concatenate([alpha0, alpha1, alpha2, alpha3, beta0, beta1, beta2, beta3], axis=1)
    outer = 1.0 / (beta2 * beta3)
    along_v = (alpha3 * alpha2 - square2) * outer
    along_u, along_w = -alpha2 * outer, -alpha3 * outer

    def last_vector(parts):
        return outer * parts[3] + along_u * parts[1] + along_w * parts[2] + along_v * parts[0]

    out[0, rep] = last_vector(mine)
    for i in range(4):
        final_copy(i).wait_recv()
    out[0, other] = last_vector(theirs)

    pltpu.make_async_copy(left, left, l_send).wait()
    pltpu.make_async_copy(right, right, r_send).wait()
    pat_copy.wait_send()
    for i in range(4):
        final_copy(i).wait_send()
    for k in range(ITERS):
        for n, d in enumerate(shifts):
            pltpu.make_async_remote_copy(
                slots[k].at[HALO], slots[k].at[HALO - d],
                halo_send.at[k, n], halo_recv.at[k, n],
                device_id=at_sector(d), device_id_type=MESH,
            ).wait_send()
    for k in range(ROUNDS):
        exchange_wait(red_z, k, nz - 1, z_send)
        exchange_wait(red_y, k, 2 * NY - 1, y_send)


def on_device(nseg, nsec, psi, left, right, block, keep_l, keep_r, pattern, charge):
    here, size = left.shape[1], left.shape[3]
    count = 2 * nsec * size * size
    nz = nsec // NY
    vmem = pl.BlockSpec(memory_space=pltpu.VMEM)
    hbm = pl.BlockSpec(memory_space=pltpu.HBM)
    square = (size, size)
    dma = pltpu.SemaphoreType.DMA
    halo = pltpu.VMEM((2 * HALO + 2, *square), BF16)
    terms = 2 * here
    return pl.pallas_call(
        functools.partial(kernel, nseg, nsec, here, size, count),
        out_shape=(
            jax.ShapeDtypeStruct(psi.shape, F32),
            jax.ShapeDtypeStruct((1, 2 * ITERS), F32),
        ),
        in_specs=[hbm] * 8,
        out_specs=(vmem, vmem),
        scratch_shapes=[
            pltpu.VMEM((terms, *square), BF16),
            pltpu.VMEM((terms, *square), BF16),
            halo, halo, halo, halo,
            pltpu.VMEM(square, F32),
            pltpu.VMEM(square, F32),
            *[pltpu.VMEM(square, F32)] * 8,
            pltpu.VMEM((4, *square), F32),
            pltpu.VMEM((4, *square), F32),
            pltpu.VMEM(square, F32),
            pltpu.VMEM(square, BF16),
            pltpu.VMEM((2, here), jnp.int32),
            pltpu.SMEM((2, 2, here), jnp.int32),
            pltpu.SMEM((1, 2), jnp.int32),
            pltpu.SMEM((1, 2), jnp.int32),
            pltpu.SMEM((terms,), jnp.int32),
            pltpu.SMEM((terms,), jnp.int32),
            pltpu.VMEM((ROUNDS, nz, SUMS, 128), F32),
            pltpu.VMEM((ROUNDS, 2 * NY, SUMS, 128), F32),
            dma((6,)), dma, dma, dma((terms,)), dma((terms,)),
            dma((ITERS, 4)), dma((ITERS, 4)),
            dma((ROUNDS,)), dma((ROUNDS,)),
            dma((ROUNDS,)), dma((ROUNDS,)),
            dma, dma, dma((4,)), dma((4,)),
        ],
        compiler_params=pltpu.CompilerParams(
            collective_id=0, has_side_effects=True, vmem_limit_bytes=60 << 20
        ),
    )(psi, left, right, block, keep_l, keep_r, jnp.transpose(pattern, (0, 2, 1)), charge)


def solution(mesh):
    placed = (
        P("seg", "sec", None, None),
        P("seg", "rep", "sec", None, None),
        P("seg", "rep", "sec", None, None),
        P("seg", "sec", None, None),
        P("seg", "sec"),
        P("seg", "sec"),
        P("seg", "rep", "sec"),
        P(),
    )
    return jax.shard_map(
        functools.partial(on_device, mesh.shape["seg"], mesh.shape["sec"]),
        mesh=mesh,
        in_specs=placed,
        out_specs=(P("seg", "sec", None, None), P("seg", None)),
        check_vma=False,
    )
```

```python
import functools

import jax
import jax.numpy as jnp
from jax import lax
from jax.experimental import pallas as pl
from jax.experimental.pallas import tpu as pltpu
from jax.sharding import PartitionSpec as P

ITERS = 4
NY = 4
HALO = 2
ROUNDS = 4
INITIAL = ROUNDS - 1
SUMS = 16
F32 = jnp.float32
BF16 = jnp.bfloat16
MESH = pl.DeviceIdType.MESH


def nt_dot(a, b):
    return lax.dot_general(a, b, (((1,), (1,)), ((), ())), preferred_element_type=F32)


def outward(n):
    return sorted(range(1, n), key=lambda i: -min(i, n - i))


def column_sums(x):
    total = jnp.sum(x, axis=0, keepdims=True)
    width = total.shape[1] // 2
    return total[:, :width] + total[:, width:]


def kernel(
    nseg, nsec, here, size, count,
    psi, left, right, block, keep_l, keep_r, pattern, charge,
    out, coeffs,
    lbuf, rbuf, vs0, vs1, vs2, vs3, acc, mask, v0, e1, e2, v1, u1, w1, hu1, hw1, mine, theirs,
    psi_v, blk_v, pat_v, pat_s, kl_s, kr_s, charge_s, index, red_z, red_y,
    load, l_send, r_send, l_recv, r_recv, halo_send, halo_recv,
    z_send, z_recv, y_send, y_recv, pat_send, pat_recv, fin_send, fin_recv,
):
    slots = (vs0, vs1, vs2, vs3)
    seg, sec, rep = lax.axis_index("seg"), lax.axis_index("sec"), lax.axis_index("rep")
    nz = nsec // NY
    z, y = sec // NY, sec % NY
    other = 1 - rep
    sector, sectors = 2 * sec + rep, 2 * nsec
    ahead, behind = (seg + 1) % nseg, (seg + nseg - 1) % nseg
    terms = 2 * here

    def at_sector(shift):
        s = (sector + sectors + shift) % sectors
        return (seg, s // 2, s % 2)

    shifts = (-1, 1, -2, 2)
    z_peers = [(seg, ((z + i) % nz) * NY + y, rep) for i in outward(nz)]
    mine_y = 2 * y + rep
    y_peers = []
    for i in outward(2 * NY):
        p = (mine_y + i) % (2 * NY)
        y_peers.append((seg, z * NY + p // 2, p % 2))

    partners = [(a, sec, jnp.int32(r)) for a in (ahead, behind) for r in range(2)]
    partners += [at_sector(d) for d in shifts] + z_peers + y_peers
    barrier = pltpu.get_barrier_semaphore()
    for p in partners:
        pl.semaphore_signal(barrier, inc=1, device_id=p, device_id_type=MESH)
    loads = [
        pltpu.make_async_copy(a, b, load.at[i])
        for i, (a, b) in enumerate([
            (psi.at[0, rep], psi_v), (block.at[0, rep], blk_v), (pattern.at[0], pat_s.at[rep]),
            (keep_l, kl_s), (keep_r, kr_s), (charge, charge_s),
        ])
    ]
    for c in loads:
        c.start()
    pl.semaphore_wait(barrier, len(partners))

    def left_copy(t, r):
        w = rep * here + t
        return pltpu.make_async_remote_copy(
            left.at[0, t, r], lbuf.at[w], l_send, l_recv.at[w],
            device_id=(ahead, sec, jnp.int32(r)), device_id_type=MESH,
        )

    def right_copy(t, r):
        w = rep * here + t
        return pltpu.make_async_remote_copy(
            right.at[0, t, r], rbuf.at[w], r_send, r_recv.at[w],
            device_id=(behind, sec, jnp.int32(r)), device_id_type=MESH,
        )

    @pl.loop(0, here)
    def _(t):
        for r in range(2):
            left_copy(t, r).start()
            right_copy(t, r).start()

    def start_halo(k):
        for n, d in enumerate(shifts):
            pltpu.make_async_remote_copy(
                slots[k].at[HALO], slots[k].at[HALO - d],
                halo_send.at[k, n], halo_recv.at[k, n],
                device_id=at_sector(d), device_id_type=MESH,
            ).start()

    def wait_halo(k):
        for n, d in enumerate(shifts):
            pltpu.make_async_remote_copy(
                slots[k].at[HALO], slots[k].at[HALO - d],
                halo_send.at[k, n], halo_recv.at[k, n],
                device_id=at_sector(d), device_id_type=MESH,
            ).wait_recv()

    def exchange_start(buf, k, mine, peers, send, recv):
        for p in peers:
            pltpu.make_async_remote_copy(
                buf.at[k, mine], buf.at[k, mine], send.at[k], recv.at[k],
                device_id=p, device_id_type=MESH,
            ).start()

    def exchange_wait(buf, k, n, sem):
        some = buf.at[k, pl.ds(0, n)]
        pltpu.make_async_copy(some, some, sem.at[k]).wait()

    def total_of(buf, k, n):
        total = buf[k, 0]
        for i in range(1, n):
            total = total + buf[k, i]
        return total

    def reduce_first(k, rows):
        red_z[k, z] = jnp.zeros_like(red_z[k, 0])
        for i, row in enumerate(rows):
            red_z[k, z, pl.ds(i, 1), :] = row
        exchange_start(red_z, k, z, z_peers, z_send, z_recv)

    def reduce_second(k):
        exchange_wait(red_z, k, nz - 1, z_recv)
        red_y[k, mine_y] = total_of(red_z, k, nz)
        exchange_start(red_y, k, mine_y, y_peers, y_send, y_recv)

    def reduce_last(k):
        exchange_wait(red_y, k, 2 * NY - 1, y_recv)
        total = jnp.sum(total_of(red_y, k, 2 * NY), axis=1, keepdims=True)
        return total * (1.0 / count)

    pat_copy = pltpu.make_async_remote_copy(
        pattern.at[0], pat_v, pat_send, pat_recv, device_id=(seg, sec, other), device_id_type=MESH
    )
    pat_copy.start()
    for c in loads:
        c.wait()

    rows = lax.broadcasted_iota(jnp.int32, (size, size), 0)
    cols = lax.broadcasted_iota(jnp.int32, (size, size), 1)
    inside = (rows < kl_s[0, rep]) & (cols < kr_s[0, rep])
    mask[...] = inside.astype(F32)
    start = mask[...] * psi_v[...]
    v0[...] = start
    reduce_first(INITIAL, [column_sums(start * start)])

    pat_copy.wait_recv()
    move = pltpu.make_async_copy(pat_v, pat_s.at[other], load.at[0])
    move.start()
    move.wait()

    for k in range(ITERS):
        slots[k][2 * HALO + 1] = jnp.zeros((size, size), BF16)

    @pl.loop(0, terms)
    def _(w):
        c = charge_s[w]
        to = sector + c
        index[w] = jnp.where((to >= 0) & (to < sectors), c + HALO, 2 * HALO + 1)

    reduce_second(INITIAL)
    scale = reduce_last(INITIAL)[0:1]
    v0[...] = v0[...] * lax.rsqrt(scale + 1e-06)
    slots[0][HALO] = v0[...].astype(BF16)
    start_halo(0)

    def apply_local(k):
        half = size // 2

        @pl.loop(0, 2)
        def _(i):
            some = pl.ds(pl.multiple_of(i * half, half), half)
            first = jnp.dot(blk_v[some, :], slots[k][HALO], preferred_element_type=F32)
            acc[some, :] = first + nt_dot(slots[k][HALO, some, :], blk_v[...])

    def term(k, q, t):
        w = q * here + t
        moved = slots[k][index[w]]
        inner = jnp.dot(lbuf[w], moved, preferred_element_type=F32)
        inner = (inner * pat_s[q, rep, t].astype(F32)).astype(BF16)
        return nt_dot(inner, rbuf[w])

    def env_wait(w):
        pltpu.make_async_remote_copy(
            left.at[0, 0, 0], lbuf.at[w], l_send, l_recv.at[w],
            device_id=(ahead, sec, rep), device_id_type=MESH,
        ).wait_recv()
        pltpu.make_async_remote_copy(
            right.at[0, 0, 0], rbuf.at[w], r_send, r_recv.at[w],
            device_id=(behind, sec, rep), device_id_type=MESH,
        ).wait_recv()

    def apply_rest(k):
        wait_halo(k)
        total = acc[...]
        for t in range(here):
            for q in range(2):
                total = total + term(k, q, t)
        acc[...] = total

    def offer(k, x):
        slots[k][HALO] = x.astype(BF16)
        start_halo(k)

    def dot(a, b):
        return column_sums(a * b)

    def coefficients(means, vu, vw, vv, ww):
        alpha = means[vu : vu + 1]
        rest = means[ww : ww + 1] - 2.0 * alpha * means[vw : vw + 1] + alpha * alpha * means[vv : vv + 1]
        return alpha, jnp.sqrt(jnp.maximum(rest, 0.0) + 1e-06)

    apply_local(0)
    wait_halo(0)

    @pl.loop(0, here)
    def _(t):
        env_wait(t)
        env_wait(here + t)
        acc[...] += term(0, 0, t) + term(0, 1, t)

    e1[...] = mask[...] * acc[...]
    offer(1, e1[...])
    reduce_first(0, [dot(v0[...], e1[...]), dot(e1[...], e1[...]), dot(v0[...], v0[...])])
    apply_local(1)
    reduce_second(0)
    apply_rest(1)

    e2[...] = mask[...] * acc[...]
    offer(2, e2[...])
    alpha0, beta0 = coefficients(reduce_last(0), 0, 0, 2, 1)
    inverse0 = 1.0 / beta0
    v1[...] = (e1[...] - alpha0 * v0[...]) * inverse0
    u1[...] = (e2[...] - alpha0 * e1[...]) * inverse0
    w1[...] = u1[...] - beta0 * v0[...]
    reduce_first(1, [dot(v1[...], u1[...]), dot(v1[...], w1[...]), dot(v1[...], v1[...]), dot(w1[...], w1[...])])
    apply_local(2)
    reduce_second(1)
    apply_rest(2)

    hu1[...] = (mask[...] * acc[...] - alpha0 * e2[...]) * inverse0
    hw1[...] = hu1[...] - beta0 * e1[...]
    offer(3, hw1[...])
    apply_local(3)
    alpha1, beta1 = coefficients(reduce_last(1), 0, 1, 2, 3)
    inverse1 = 1.0 / beta1
    mine[0] = (w1[...] - alpha1 * v1[...]) * inverse1
    mine[1] = (hw1[...] - alpha1 * u1[...]) * inverse1
    mine[2] = mine[1] - beta1 * v1[...]

    def final_copy(i):
        return pltpu.make_async_remote_copy(
            mine.at[i], theirs.at[i], fin_send.at[i], fin_recv.at[i],
            device_id=(seg, sec, other), device_id_type=MESH,
        )

    for i in range(3):
        final_copy(i).start()
    hu1[...] = alpha1 * hu1[...] + beta1 * beta1 * u1[...]
    v2, u2, w2 = mine[0], mine[1], mine[2]
    early = [dot(v2, u2), dot(v2, w2), dot(v2, v2), dot(w2, w2), dot(w2, u2), dot(u2, u2)]
    apply_rest(3)

    mine[3] = (mask[...] * acc[...] - hu1[...]) * inverse1
    h, v2, u2, w2 = mine[3], mine[0], mine[1], mine[2]
    reduce_first(2, early + [dot(w2, h), dot(v2, h), dot(h, h), dot(u2, h)])
    final_copy(3).start()
    reduce_second(2)
    means = reduce_last(2)
    vu, vw, vv, ww, wu, uu, wh, vh, hh, uh = (means[i : i + 1] for i in range(10))
    alpha2, beta2 = coefficients(means, 0, 1, 2, 3)
    square2 = beta2 * beta2
    inverse2 = 1.0 / square2
    alpha3 = (wh - alpha2 * (wu + vh) + alpha2 * alpha2 * vu) * inverse2
    ww3 = (
        hh + alpha2 * alpha2 * uu + square2 * square2 * vv
        - 2.0 * (alpha2 * uh + square2 * vh) + 2.0 * alpha2 * square2 * vu
    ) * inverse2
    vv3 = (ww - 2.0 * alpha2 * vw + alpha2 * alpha2 * vv) * inverse2
    vw3 = alpha3 - vw + alpha2 * vv
    rest = ww3 - 2.0 * alpha3 * vw3 + alpha3 * alpha3 * vv3
    beta3 = jnp.sqrt(jnp.maximum(rest, 0.0) + 1e-06)
    coeffs[...] = jnp.concatenate([alpha0, alpha1, alpha2, alpha3, beta0, beta1, beta2, beta3], axis=1)
    outer = 1.0 / (beta2 * beta3)
    along_v = (alpha3 * alpha2 - square2) * outer
    along_u, along_w = -alpha2 * outer, -alpha3 * outer

    def last_vector(parts):
        return outer * parts[3] + along_u * parts[1] + along_w * parts[2] + along_v * parts[0]

    out[0, rep] = last_vector(mine)
    for i in range(4):
        final_copy(i).wait_recv()
    out[0, other] = last_vector(theirs)

    pltpu.make_async_copy(left, left, l_send).wait()
    pltpu.make_async_copy(right, right, r_send).wait()
    pat_copy.wait_send()
    for i in range(4):
        final_copy(i).wait_send()
    for k in range(ITERS):
        for n, d in enumerate(shifts):
            pltpu.make_async_remote_copy(
                slots[k].at[HALO], slots[k].at[HALO - d],
                halo_send.at[k, n], halo_recv.at[k, n],
                device_id=at_sector(d), device_id_type=MESH,
            ).wait_send()
    for k in range(ROUNDS):
        exchange_wait(red_z, k, nz - 1, z_send)
        exchange_wait(red_y, k, 2 * NY - 1, y_send)


def on_device(nseg, nsec, psi, left, right, block, keep_l, keep_r, pattern, charge):
    here, size = left.shape[1], left.shape[3]
    count = 2 * nsec * size * size
    nz = nsec // NY
    vmem = pl.BlockSpec(memory_space=pltpu.VMEM)
    hbm = pl.BlockSpec(memory_space=pltpu.HBM)
    square = (size, size)
    dma = pltpu.SemaphoreType.DMA
    halo = pltpu.VMEM((2 * HALO + 2, *square), BF16)
    terms = 2 * here
    return pl.pallas_call(
        functools.partial(kernel, nseg, nsec, here, size, count),
        out_shape=(
            jax.ShapeDtypeStruct(psi.shape, F32),
            jax.ShapeDtypeStruct((1, 2 * ITERS), F32),
        ),
        in_specs=[hbm] * 8,
        out_specs=(vmem, vmem),
        scratch_shapes=[
            pltpu.VMEM((terms, *square), BF16),
            pltpu.VMEM((terms, *square), BF16),
            halo, halo, halo, halo,
            pltpu.VMEM(square, F32),
            pltpu.VMEM(square, F32),
            *[pltpu.VMEM(square, F32)] * 8,
            pltpu.VMEM((4, *square), F32),
            pltpu.VMEM((4, *square), F32),
            pltpu.VMEM(square, F32),
            pltpu.VMEM(square, BF16),
            pltpu.VMEM((2, here), jnp.int32),
            pltpu.SMEM((2, 2, here), jnp.int32),
            pltpu.SMEM((1, 2), jnp.int32),
            pltpu.SMEM((1, 2), jnp.int32),
            pltpu.SMEM((terms,), jnp.int32),
            pltpu.SMEM((terms,), jnp.int32),
            pltpu.VMEM((ROUNDS, nz, SUMS, 128), F32),
            pltpu.VMEM((ROUNDS, 2 * NY, SUMS, 128), F32),
            dma((6,)), dma, dma, dma((terms,)), dma((terms,)),
            dma((ITERS, 4)), dma((ITERS, 4)),
            dma((ROUNDS,)), dma((ROUNDS,)),
            dma((ROUNDS,)), dma((ROUNDS,)),
            dma, dma, dma((4,)), dma((4,)),
        ],
        compiler_params=pltpu.CompilerParams(
            collective_id=0, has_side_effects=True, vmem_limit_bytes=60 << 20
        ),
    )(psi, left, right, block, keep_l, keep_r, jnp.transpose(pattern, (0, 2, 1)), charge)


def solution(mesh):
    placed = (
        P("seg", "sec", None, None),
        P("seg", "rep", "sec", None, None),
        P("seg", "rep", "sec", None, None),
        P("seg", "sec", None, None),
        P("seg", "sec"),
        P("seg", "sec"),
        P("seg", "rep", "sec"),
        P(),
    )
    return jax.shard_map(
        functools.partial(on_device, mesh.shape["seg"], mesh.shape["sec"]),
        mesh=mesh,
        in_specs=placed,
        out_specs=(P("seg", "sec", None, None), P("seg", None)),
        check_vma=False,
    )
```

```python
import functools

import jax
import jax.numpy as jnp
from jax import lax
from jax.experimental import pallas as pl
from jax.experimental.pallas import tpu as pltpu
from jax.sharding import PartitionSpec as P

ITERS = 4
NY = 4
HALO = 2
ROUNDS = 4
INITIAL = ROUNDS - 1
SUMS = 16
F32 = jnp.float32
BF16 = jnp.bfloat16
MESH = pl.DeviceIdType.MESH


def nt_dot(a, b):
    return lax.dot_general(a, b, (((1,), (1,)), ((), ())), preferred_element_type=F32)


def outward(n):
    return sorted(range(1, n), key=lambda i: -min(i, n - i))


def column_sums(x):
    total = jnp.sum(x, axis=0, keepdims=True)
    width = total.shape[1] // 2
    return total[:, :width] + total[:, width:]


def kernel(
    nseg, nsec, here, size, count,
    psi, left, right, block, keep_l, keep_r, pattern, charge,
    out, coeffs,
    lbuf, rbuf, vs0, vs1, vs2, vs3, acc, mask, v0, e1, e2, v1, u1, w1, hu1, hw1, mine, theirs,
    psi_v, blk_v, pat_v, pat_s, kl_s, kr_s, charge_s, index, red_z, red_y,
    load, l_send, r_send, l_recv, r_recv, halo_send, halo_recv,
    z_send, z_recv, y_send, y_recv, pat_send, pat_recv, fin_send, fin_recv,
):
    slots = (vs0, vs1, vs2, vs3)
    seg, sec, rep = lax.axis_index("seg"), lax.axis_index("sec"), lax.axis_index("rep")
    nz = nsec // NY
    z, y = sec // NY, sec % NY
    other = 1 - rep
    sector, sectors = 2 * sec + rep, 2 * nsec
    ahead, behind = (seg + 1) % nseg, (seg + nseg - 1) % nseg
    terms = 2 * here

    def at_sector(shift):
        s = (sector + sectors + shift) % sectors
        return (seg, s // 2, s % 2)

    sign = 2 * rep - 1
    shifts = (sign, 2 * sign, -2 * sign, -sign)
    z_peers = [(seg, ((z + i) % nz) * NY + y, rep) for i in outward(nz)]
    mine_y = 2 * y + rep
    y_peers = []
    for i in outward(2 * NY):
        p = (mine_y + i) % (2 * NY)
        y_peers.append((seg, z * NY + p // 2, p % 2))

    partners = [(a, sec, jnp.int32(r)) for a in (ahead, behind) for r in range(2)]
    partners += [at_sector(d) for d in shifts] + z_peers + y_peers
    barrier = pltpu.get_barrier_semaphore()
    for p in partners:
        pl.semaphore_signal(barrier, inc=1, device_id=p, device_id_type=MESH)
    loads = [
        pltpu.make_async_copy(a, b, load.at[i])
        for i, (a, b) in enumerate([
            (psi.at[0, rep], psi_v), (block.at[0, rep], blk_v), (pattern.at[0], pat_s.at[rep]),
            (keep_l, kl_s), (keep_r, kr_s), (charge, charge_s),
        ])
    ]
    for c in loads:
        c.start()
    pl.semaphore_wait(barrier, len(partners))

    def left_copy(t, r):
        w = rep * here + t
        return pltpu.make_async_remote_copy(
            left.at[0, t, r], lbuf.at[w], l_send, l_recv.at[w],
            device_id=(ahead, sec, jnp.int32(r)), device_id_type=MESH,
        )

    def right_copy(t, r):
        w = rep * here + t
        return pltpu.make_async_remote_copy(
            right.at[0, t, r], rbuf.at[w], r_send, r_recv.at[w],
            device_id=(behind, sec, jnp.int32(r)), device_id_type=MESH,
        )

    @pl.loop(0, here)
    def _(t):
        for r in range(2):
            left_copy(t, r).start()
            right_copy(t, r).start()

    def start_halo(k):
        for n, d in enumerate(shifts):
            pltpu.make_async_remote_copy(
                slots[k].at[HALO], slots[k].at[HALO - d],
                halo_send.at[k, n], halo_recv.at[k, n],
                device_id=at_sector(d), device_id_type=MESH,
            ).start()

    def wait_halo(k):
        for n, d in enumerate(shifts):
            pltpu.make_async_remote_copy(
                slots[k].at[HALO], slots[k].at[HALO - d],
                halo_send.at[k, n], halo_recv.at[k, n],
                device_id=at_sector(d), device_id_type=MESH,
            ).wait_recv()

    def exchange_start(buf, k, mine, peers, send, recv):
        for p in peers:
            pltpu.make_async_remote_copy(
                buf.at[k, mine], buf.at[k, mine], send.at[k], recv.at[k],
                device_id=p, device_id_type=MESH,
            ).start()

    def exchange_wait(buf, k, n, sem):
        some = buf.at[k, pl.ds(0, n)]
        pltpu.make_async_copy(some, some, sem.at[k]).wait()

    def total_of(buf, k, n):
        total = buf[k, 0]
        for i in range(1, n):
            total = total + buf[k, i]
        return total

    lanes = lax.broadcasted_iota(jnp.int32, (SUMS, 128), 1)
    diagonal = lanes == lax.broadcasted_iota(jnp.int32, (SUMS, 128), 0)

    def reduce_first(k, rows):
        rows = rows + [jnp.zeros((SUMS - len(rows), 128), F32)]
        sums = jnp.sum(jnp.concatenate(rows, axis=0), axis=1, keepdims=True)
        red_z[k, z] = jnp.sum(jnp.where(diagonal, sums, 0.0), axis=0, keepdims=True)
        exchange_start(red_z, k, z, z_peers, z_send, z_recv)

    def reduce_second(k):
        exchange_wait(red_z, k, nz - 1, z_recv)
        red_y[k, mine_y] = total_of(red_z, k, nz)
        exchange_start(red_y, k, mine_y, y_peers, y_send, y_recv)

    def reduce_last(k):
        exchange_wait(red_y, k, 2 * NY - 1, y_recv)
        total = jnp.where(diagonal, total_of(red_y, k, 2 * NY), 0.0)
        return jnp.sum(total, axis=1, keepdims=True) * (1.0 / count)

    pat_copy = pltpu.make_async_remote_copy(
        pattern.at[0], pat_v, pat_send, pat_recv, device_id=(seg, sec, other), device_id_type=MESH
    )
    pat_copy.start()
    for c in loads:
        c.wait()

    rows = lax.broadcasted_iota(jnp.int32, (size, size), 0)
    cols = lax.broadcasted_iota(jnp.int32, (size, size), 1)
    inside = (rows < kl_s[0, rep]) & (cols < kr_s[0, rep])
    mask[...] = inside.astype(F32)
    start = mask[...] * psi_v[...]
    v0[...] = start
    reduce_first(INITIAL, [column_sums(start * start)])

    pat_copy.wait_recv()
    move = pltpu.make_async_copy(pat_v, pat_s.at[other], load.at[0])
    move.start()
    move.wait()

    for k in range(ITERS):
        slots[k][2 * HALO + 1] = jnp.zeros((size, size), BF16)

    @pl.loop(0, terms)
    def _(w):
        c = charge_s[w]
        to = sector + c
        index[w] = jnp.where((to >= 0) & (to < sectors), c + HALO, 2 * HALO + 1)

    reduce_second(INITIAL)
    scale = reduce_last(INITIAL)[0:1]
    v0[...] = v0[...] * lax.rsqrt(scale + 1e-06)
    slots[0][HALO] = v0[...].astype(BF16)
    start_halo(0)

    def apply_local(k):
        half = size // 2

        @pl.loop(0, 2)
        def _(i):
            some = pl.ds(pl.multiple_of(i * half, half), half)
            first = jnp.dot(blk_v[some, :], slots[k][HALO], preferred_element_type=F32)
            acc[some, :] = first + nt_dot(slots[k][HALO, some, :], blk_v[...])

    def term(k, q, t):
        w = q * here + t
        moved = slots[k][index[w]]
        inner = jnp.dot(lbuf[w], moved, preferred_element_type=F32)
        inner = (inner * pat_s[q, rep, t].astype(F32)).astype(BF16)
        return nt_dot(inner, rbuf[w])

    def env_wait(w):
        pltpu.make_async_remote_copy(
            left.at[0, 0, 0], lbuf.at[w], l_send, l_recv.at[w],
            device_id=(ahead, sec, rep), device_id_type=MESH,
        ).wait_recv()
        pltpu.make_async_remote_copy(
            right.at[0, 0, 0], rbuf.at[w], r_send, r_recv.at[w],
            device_id=(behind, sec, rep), device_id_type=MESH,
        ).wait_recv()

    def apply_rest(k):
        wait_halo(k)
        total = acc[...]
        for t in range(here):
            for q in range(2):
                total = total + term(k, q, t)
        acc[...] = total

    def offer(k, x):
        slots[k][HALO] = x.astype(BF16)
        start_halo(k)

    def dot(a, b):
        return column_sums(a * b)

    def coefficients(means, vu, vw, vv, ww):
        alpha = means[vu : vu + 1]
        rest = means[ww : ww + 1] - 2.0 * alpha * means[vw : vw + 1] + alpha * alpha * means[vv : vv + 1]
        return alpha, jnp.sqrt(jnp.maximum(rest, 0.0) + 1e-06)

    apply_local(0)
    wait_halo(0)

    @pl.loop(0, here)
    def _(t):
        env_wait(t)
        env_wait(here + t)
        acc[...] += term(0, 0, t) + term(0, 1, t)

    e1[...] = mask[...] * acc[...]
    offer(1, e1[...])
    reduce_first(0, [dot(v0[...], e1[...]), dot(e1[...], e1[...]), dot(v0[...], v0[...])])
    apply_local(1)
    reduce_second(0)
    apply_rest(1)

    e2[...] = mask[...] * acc[...]
    offer(2, e2[...])
    alpha0, beta0 = coefficients(reduce_last(0), 0, 0, 2, 1)
    inverse0 = 1.0 / beta0
    v1[...] = (e1[...] - alpha0 * v0[...]) * inverse0
    u1[...] = (e2[...] - alpha0 * e1[...]) * inverse0
    w1[...] = u1[...] - beta0 * v0[...]
    reduce_first(1, [dot(v1[...], u1[...]), dot(v1[...], w1[...]), dot(v1[...], v1[...]), dot(w1[...], w1[...])])
    apply_local(2)
    reduce_second(1)
    apply_rest(2)

    hu1[...] = (mask[...] * acc[...] - alpha0 * e2[...]) * inverse0
    hw1[...] = hu1[...] - beta0 * e1[...]
    offer(3, hw1[...])
    apply_local(3)
    alpha1, beta1 = coefficients(reduce_last(1), 0, 1, 2, 3)
    inverse1 = 1.0 / beta1
    mine[0] = (w1[...] - alpha1 * v1[...]) * inverse1
    mine[1] = (hw1[...] - alpha1 * u1[...]) * inverse1
    mine[2] = mine[1] - beta1 * v1[...]

    def final_copy(i):
        return pltpu.make_async_remote_copy(
            mine.at[i], theirs.at[i], fin_send.at[i], fin_recv.at[i],
            device_id=(seg, sec, other), device_id_type=MESH,
        )

    for i in range(3):
        final_copy(i).start()
    hu1[...] = alpha1 * hu1[...] + beta1 * beta1 * u1[...]
    v2, u2, w2 = mine[0], mine[1], mine[2]
    early = [dot(v2, u2), dot(v2, w2), dot(v2, v2), dot(w2, w2), dot(w2, u2), dot(u2, u2)]
    apply_rest(3)

    mine[3] = (mask[...] * acc[...] - hu1[...]) * inverse1
    h, v2, u2, w2 = mine[3], mine[0], mine[1], mine[2]
    reduce_first(2, early + [dot(w2, h), dot(v2, h), dot(h, h), dot(u2, h)])
    final_copy(3).start()
    reduce_second(2)
    means = reduce_last(2)
    vu, vw, vv, ww, wu, uu, wh, vh, hh, uh = (means[i : i + 1] for i in range(10))
    alpha2, beta2 = coefficients(means, 0, 1, 2, 3)
    square2 = beta2 * beta2
    inverse2 = 1.0 / square2
    alpha3 = (wh - alpha2 * (wu + vh) + alpha2 * alpha2 * vu) * inverse2
    ww3 = (
        hh + alpha2 * alpha2 * uu + square2 * square2 * vv
        - 2.0 * (alpha2 * uh + square2 * vh) + 2.0 * alpha2 * square2 * vu
    ) * inverse2
    vv3 = (ww - 2.0 * alpha2 * vw + alpha2 * alpha2 * vv) * inverse2
    vw3 = alpha3 - vw + alpha2 * vv
    rest = ww3 - 2.0 * alpha3 * vw3 + alpha3 * alpha3 * vv3
    beta3 = jnp.sqrt(jnp.maximum(rest, 0.0) + 1e-06)
    coeffs[...] = jnp.concatenate([alpha0, alpha1, alpha2, alpha3, beta0, beta1, beta2, beta3], axis=1)
    outer = 1.0 / (beta2 * beta3)
    along_v = (alpha3 * alpha2 - square2) * outer
    along_u, along_w = -alpha2 * outer, -alpha3 * outer

    def last_vector(parts):
        return outer * parts[3] + along_u * parts[1] + along_w * parts[2] + along_v * parts[0]

    out[0, rep] = last_vector(mine)
    for i in range(4):
        final_copy(i).wait_recv()
    out[0, other] = last_vector(theirs)

    pltpu.make_async_copy(left, left, l_send).wait()
    pltpu.make_async_copy(right, right, r_send).wait()
    pat_copy.wait_send()
    for i in range(4):
        final_copy(i).wait_send()
    for k in range(ITERS):
        for n, d in enumerate(shifts):
            pltpu.make_async_remote_copy(
                slots[k].at[HALO], slots[k].at[HALO - d],
                halo_send.at[k, n], halo_recv.at[k, n],
                device_id=at_sector(d), device_id_type=MESH,
            ).wait_send()
    for k in range(ROUNDS):
        exchange_wait(red_z, k, nz - 1, z_send)
        exchange_wait(red_y, k, 2 * NY - 1, y_send)


def on_device(nseg, nsec, psi, left, right, block, keep_l, keep_r, pattern, charge):
    here, size = left.shape[1], left.shape[3]
    count = 2 * nsec * size * size
    nz = nsec // NY
    pin = lambda x: pltpu.with_memory_space_constraint(x, pltpu.HBM)
    vmem = pl.BlockSpec(memory_space=pltpu.VMEM)
    hbm = pl.BlockSpec(memory_space=pltpu.HBM)
    square = (size, size)
    dma = pltpu.SemaphoreType.DMA
    halo = pltpu.VMEM((2 * HALO + 2, *square), BF16)
    terms = 2 * here
    return pl.pallas_call(
        functools.partial(kernel, nseg, nsec, here, size, count),
        out_shape=(
            jax.ShapeDtypeStruct(psi.shape, F32),
            jax.ShapeDtypeStruct((1, 2 * ITERS), F32),
        ),
        in_specs=[hbm] * 8,
        out_specs=(vmem, vmem),
        scratch_shapes=[
            pltpu.VMEM((terms, *square), BF16),
            pltpu.VMEM((terms, *square), BF16),
            halo, halo, halo, halo,
            pltpu.VMEM(square, F32),
            pltpu.VMEM(square, F32),
            *[pltpu.VMEM(square, F32)] * 8,
            pltpu.VMEM((4, *square), F32),
            pltpu.VMEM((4, *square), F32),
            pltpu.VMEM(square, F32),
            pltpu.VMEM(square, BF16),
            pltpu.VMEM((2, here), jnp.int32),
            pltpu.SMEM((2, 2, here), jnp.int32),
            pltpu.SMEM((1, 2), jnp.int32),
            pltpu.SMEM((1, 2), jnp.int32),
            pltpu.SMEM((terms,), jnp.int32),
            pltpu.SMEM((terms,), jnp.int32),
            pltpu.VMEM((ROUNDS, nz, 1, 128), F32),
            pltpu.VMEM((ROUNDS, 2 * NY, 1, 128), F32),
            dma((6,)), dma, dma, dma((terms,)), dma((terms,)),
            dma((ITERS, 4)), dma((ITERS, 4)),
            dma((ROUNDS,)), dma((ROUNDS,)),
            dma((ROUNDS,)), dma((ROUNDS,)),
            dma, dma, dma((4,)), dma((4,)),
        ],
        compiler_params=pltpu.CompilerParams(
            collective_id=0, has_side_effects=True, vmem_limit_bytes=48 << 20
        ),
    )(*map(pin, (psi, left, right, block, keep_l, keep_r, jnp.transpose(pattern, (0, 2, 1)), charge)))


def solution(mesh):
    placed = (
        P("seg", "sec", None, None),
        P("seg", "rep", "sec", None, None),
        P("seg", "rep", "sec", None, None),
        P("seg", "sec", None, None),
        P("seg", "sec"),
        P("seg", "sec"),
        P("seg", "rep", "sec"),
        P(),
    )
    return jax.shard_map(
        functools.partial(on_device, mesh.shape["seg"], mesh.shape["sec"]),
        mesh=mesh,
        in_specs=placed,
        out_specs=(P("seg", "sec", None, None), P("seg", None)),
        check_vma=False,
    )
```

```python
import functools

import jax
import jax.numpy as jnp
from jax import lax
from jax.experimental import pallas as pl
from jax.experimental.pallas import tpu as pltpu
from jax.sharding import PartitionSpec as P

ITERS = 4
NY = 4
HALO = 2
ROUNDS = 4
INITIAL = ROUNDS - 1
SUMS = 16
F32 = jnp.float32
BF16 = jnp.bfloat16
MESH = pl.DeviceIdType.MESH


def nt_dot(a, b):
    return lax.dot_general(a, b, (((1,), (1,)), ((), ())), preferred_element_type=F32)


def outward(n):
    return sorted(range(1, n), key=lambda i: -min(i, n - i))


def column_sums(x):
    total = jnp.sum(x, axis=0, keepdims=True)
    width = total.shape[1] // 2
    return total[:, :width] + total[:, width:]


def kernel(
    nseg, nsec, here, size, count,
    psi, left, right, block, keep_l, keep_r, pattern, charge,
    out, coeffs,
    lbuf, rbuf, vs0, vs1, vs2, vs3, acc, mask, v0, e1, e2, v1, u1, w1, hu1, hw1, mine, theirs,
    psi_v, blk_v, pat_v, pat_s, kl_s, kr_s, charge_s, index, red_z, red_y,
    near_sem, far_sem, load, l_send, r_send, l_recv, r_recv, halo_send, halo_recv,
    z_send, z_recv, y_send, y_recv, pat_send, pat_recv, fin_send, fin_recv,
):
    slots = (vs0, vs1, vs2, vs3)
    seg, sec, rep = lax.axis_index("seg"), lax.axis_index("sec"), lax.axis_index("rep")
    nz = nsec // NY
    z, y = sec // NY, sec % NY
    other = 1 - rep
    sector, sectors = 2 * sec + rep, 2 * nsec
    ahead, behind = (seg + 1) % nseg, (seg + nseg - 1) % nseg
    terms = 2 * here

    def at_sector(shift):
        s = (sector + sectors + shift) % sectors
        return (seg, s // 2, s % 2)

    sign = 2 * rep - 1
    shifts = (sign, 2 * sign, -2 * sign, -sign)
    z_peers = [(seg, ((z + i) % nz) * NY + y, rep) for i in outward(nz)]
    mine_y = 2 * y + rep
    y_peers = []
    for i in outward(2 * NY):
        p = (mine_y + i) % (2 * NY)
        y_peers.append((seg, z * NY + p // 2, p % 2))

    def at_yz(dy, dz, r):
        return (seg, ((z + nz + dz) % nz) * NY + (y + NY + dy) % NY, r)

    partners = [(a, sec, jnp.int32(r)) for a in (ahead, behind) for r in range(2)]
    partners += [at_yz(0, d, rep) for d in (-1, 1)]
    partners += [at_yz(d, 0, jnp.int32(r)) for d in (-1, 1) for r in range(2)]
    partners += [(seg, sec, other)]
    barrier = pltpu.get_barrier_semaphore()
    for p in partners:
        pl.semaphore_signal(barrier, inc=1, device_id=p, device_id_type=MESH)
    loads = [
        pltpu.make_async_copy(a, b, load.at[i])
        for i, (a, b) in enumerate([
            (psi.at[0, rep], psi_v), (block.at[0, rep], blk_v), (pattern.at[0], pat_s.at[rep]),
            (keep_l, kl_s), (keep_r, kr_s), (charge, charge_s),
        ])
    ]
    for c in loads:
        c.start()
    pl.semaphore_wait(barrier, len(partners))

    def left_copy(t, r):
        w = rep * here + t
        return pltpu.make_async_remote_copy(
            left.at[0, t, r], lbuf.at[w], l_send, l_recv.at[w],
            device_id=(ahead, sec, r), device_id_type=MESH,
        )

    def right_copy(t, r):
        w = rep * here + t
        return pltpu.make_async_remote_copy(
            right.at[0, t, r], rbuf.at[w], r_send, r_recv.at[w],
            device_id=(behind, sec, r), device_id_type=MESH,
        )

    for i in range(2):
        @pl.loop(0, here)
        def _(t):
            left_copy(t, (sec + i) % 2).start()
            right_copy(t, (sec + i) % 2).start()

    def start_halo(k):
        for n, d in enumerate(shifts):
            pltpu.make_async_remote_copy(
                slots[k].at[HALO], slots[k].at[HALO - d],
                halo_send.at[k, n], halo_recv.at[k, n],
                device_id=at_sector(d), device_id_type=MESH,
            ).start()

    def wait_halo(k):
        for n, d in enumerate(shifts):
            pltpu.make_async_remote_copy(
                slots[k].at[HALO], slots[k].at[HALO - d],
                halo_send.at[k, n], halo_recv.at[k, n],
                device_id=at_sector(d), device_id_type=MESH,
            ).wait_recv()

    def exchange_start(buf, k, mine, peers, send, recv):
        for p in peers:
            pltpu.make_async_remote_copy(
                buf.at[k, mine], buf.at[k, mine], send.at[k], recv.at[k],
                device_id=p, device_id_type=MESH,
            ).start()

    def exchange_wait(buf, k, n, sem):
        some = buf.at[k, pl.ds(0, n)]
        pltpu.make_async_copy(some, some, sem.at[k]).wait()

    def total_of(buf, k, n):
        total = buf[k, 0]
        for i in range(1, n):
            total = total + buf[k, i]
        return total

    lanes = lax.broadcasted_iota(jnp.int32, (SUMS, 128), 1)
    diagonal = lanes == lax.broadcasted_iota(jnp.int32, (SUMS, 128), 0)

    def reduce_first(k, rows):
        rows = rows + [jnp.zeros((SUMS - len(rows), 128), F32)]
        sums = jnp.sum(jnp.concatenate(rows, axis=0), axis=1, keepdims=True)
        red_z[k, z] = jnp.sum(jnp.where(diagonal, sums, 0.0), axis=0, keepdims=True)
        exchange_start(red_z, k, z, z_peers, z_send, z_recv)

    def reduce_second(k):
        exchange_wait(red_z, k, nz - 1, z_recv)
        red_y[k, mine_y] = total_of(red_z, k, nz)
        exchange_start(red_y, k, mine_y, y_peers, y_send, y_recv)

    def reduce_last(k):
        exchange_wait(red_y, k, 2 * NY - 1, y_recv)
        total = jnp.where(diagonal, total_of(red_y, k, 2 * NY), 0.0)
        return jnp.sum(total, axis=1, keepdims=True) * (1.0 / count)

    near = [at_yz(0, d, rep) for d in (-1, 1)] + [at_yz(d, 0, rep) for d in (-1, 1)]
    for p in near:
        pl.semaphore_signal(near_sem, inc=1, device_id=p, device_id_type=MESH)
    pl.semaphore_wait(near_sem, len(near))
    far = [at_yz(0, d, rep) for d in (-2, 2)]
    for p in far:
        pl.semaphore_signal(far_sem, inc=1, device_id=p, device_id_type=MESH)
    pl.semaphore_wait(far_sem, len(far))

    pat_copy = pltpu.make_async_remote_copy(
        pattern.at[0], pat_v, pat_send, pat_recv, device_id=(seg, sec, other), device_id_type=MESH
    )
    pat_copy.start()
    for c in loads:
        c.wait()

    rows = lax.broadcasted_iota(jnp.int32, (size, size), 0)
    cols = lax.broadcasted_iota(jnp.int32, (size, size), 1)
    inside = (rows < kl_s[0, rep]) & (cols < kr_s[0, rep])
    mask[...] = inside.astype(F32)
    start = mask[...] * psi_v[...]
    v0[...] = start
    reduce_first(INITIAL, [column_sums(start * start)])

    pat_copy.wait_recv()
    move = pltpu.make_async_copy(pat_v, pat_s.at[other], load.at[0])
    move.start()
    move.wait()

    for k in range(ITERS):
        slots[k][2 * HALO + 1] = jnp.zeros((size, size), BF16)

    @pl.loop(0, terms)
    def _(w):
        c = charge_s[w]
        to = sector + c
        index[w] = jnp.where((to >= 0) & (to < sectors), c + HALO, 2 * HALO + 1)

    reduce_second(INITIAL)
    scale = reduce_last(INITIAL)[0:1]
    v0[...] = v0[...] * lax.rsqrt(scale + 1e-06)
    slots[0][HALO] = v0[...].astype(BF16)
    start_halo(0)

    def apply_local(k):
        half = size // 2

        @pl.loop(0, 2)
        def _(i):
            some = pl.ds(pl.multiple_of(i * half, half), half)
            first = jnp.dot(blk_v[some, :], slots[k][HALO], preferred_element_type=F32)
            acc[some, :] = first + nt_dot(slots[k][HALO, some, :], blk_v[...])

    def term(k, q, t):
        w = q * here + t
        moved = slots[k][index[w]]
        inner = jnp.dot(lbuf[w], moved, preferred_element_type=F32)
        inner = (inner * pat_s[q, rep, t].astype(F32)).astype(BF16)
        return nt_dot(inner, rbuf[w])

    def env_wait(w):
        pltpu.make_async_remote_copy(
            left.at[0, 0, 0], lbuf.at[w], l_send, l_recv.at[w],
            device_id=(ahead, sec, rep), device_id_type=MESH,
        ).wait_recv()
        pltpu.make_async_remote_copy(
            right.at[0, 0, 0], rbuf.at[w], r_send, r_recv.at[w],
            device_id=(behind, sec, rep), device_id_type=MESH,
        ).wait_recv()

    def apply_rest(k):
        wait_halo(k)
        total = acc[...]
        for t in range(here):
            for q in range(2):
                total = total + term(k, q, t)
        acc[...] = total

    def offer(k, x):
        slots[k][HALO] = x.astype(BF16)
        start_halo(k)

    def dot(a, b):
        return column_sums(a * b)

    def coefficients(means, vu, vw, vv, ww):
        alpha = means[vu : vu + 1]
        rest = means[ww : ww + 1] - 2.0 * alpha * means[vw : vw + 1] + alpha * alpha * means[vv : vv + 1]
        return alpha, jnp.sqrt(jnp.maximum(rest, 0.0) + 1e-06)

    apply_local(0)
    wait_halo(0)

    @pl.loop(0, here)
    def _(t):
        env_wait(t)
        env_wait(here + t)
        acc[...] += term(0, 0, t) + term(0, 1, t)

    e1[...] = mask[...] * acc[...]
    offer(1, e1[...])
    reduce_first(0, [dot(v0[...], e1[...]), dot(e1[...], e1[...]), dot(v0[...], v0[...])])
    apply_local(1)
    reduce_second(0)
    apply_rest(1)

    e2[...] = mask[...] * acc[...]
    offer(2, e2[...])
    alpha0, beta0 = coefficients(reduce_last(0), 0, 0, 2, 1)
    inverse0 = 1.0 / beta0
    v1[...] = (e1[...] - alpha0 * v0[...]) * inverse0
    u1[...] = (e2[...] - alpha0 * e1[...]) * inverse0
    w1[...] = u1[...] - beta0 * v0[...]
    reduce_first(1, [dot(v1[...], u1[...]), dot(v1[...], w1[...]), dot(v1[...], v1[...]), dot(w1[...], w1[...])])
    apply_local(2)
    reduce_second(1)
    apply_rest(2)

    hu1[...] = (mask[...] * acc[...] - alpha0 * e2[...]) * inverse0
    hw1[...] = hu1[...] - beta0 * e1[...]
    offer(3, hw1[...])
    apply_local(3)
    alpha1, beta1 = coefficients(reduce_last(1), 0, 1, 2, 3)
    inverse1 = 1.0 / beta1
    mine[0] = (w1[...] - alpha1 * v1[...]) * inverse1
    mine[1] = (hw1[...] - alpha1 * u1[...]) * inverse1
    mine[2] = mine[1] - beta1 * v1[...]

    def final_copy(i):
        return pltpu.make_async_remote_copy(
            mine.at[i], theirs.at[i], fin_send.at[i], fin_recv.at[i],
            device_id=(seg, sec, other), device_id_type=MESH,
        )

    for i in range(3):
        final_copy(i).start()
    hu1[...] = alpha1 * hu1[...] + beta1 * beta1 * u1[...]
    v2, u2, w2 = mine[0], mine[1], mine[2]
    early = [dot(v2, u2), dot(v2, w2), dot(v2, v2), dot(w2, w2), dot(w2, u2), dot(u2, u2)]
    apply_rest(3)

    mine[3] = (mask[...] * acc[...] - hu1[...]) * inverse1
    h, v2, u2, w2 = mine[3], mine[0], mine[1], mine[2]
    reduce_first(2, early + [dot(w2, h), dot(v2, h), dot(h, h), dot(u2, h)])
    final_copy(3).start()
    reduce_second(2)
    means = reduce_last(2)
    vu, vw, vv, ww, wu, uu, wh, vh, hh, uh = (means[i : i + 1] for i in range(10))
    alpha2, beta2 = coefficients(means, 0, 1, 2, 3)
    square2 = beta2 * beta2
    inverse2 = 1.0 / square2
    alpha3 = (wh - alpha2 * (wu + vh) + alpha2 * alpha2 * vu) * inverse2
    ww3 = (
        hh + alpha2 * alpha2 * uu + square2 * square2 * vv
        - 2.0 * (alpha2 * uh + square2 * vh) + 2.0 * alpha2 * square2 * vu
    ) * inverse2
    vv3 = (ww - 2.0 * alpha2 * vw + alpha2 * alpha2 * vv) * inverse2
    vw3 = alpha3 - vw + alpha2 * vv
    rest = ww3 - 2.0 * alpha3 * vw3 + alpha3 * alpha3 * vv3
    beta3 = jnp.sqrt(jnp.maximum(rest, 0.0) + 1e-06)
    coeffs[...] = jnp.concatenate([alpha0, alpha1, alpha2, alpha3, beta0, beta1, beta2, beta3], axis=1)
    outer = 1.0 / (beta2 * beta3)
    along_v = (alpha3 * alpha2 - square2) * outer
    along_u, along_w = -alpha2 * outer, -alpha3 * outer

    def last_vector(parts):
        return outer * parts[3] + along_u * parts[1] + along_w * parts[2] + along_v * parts[0]

    out[0, rep] = last_vector(mine)
    for i in range(4):
        final_copy(i).wait_recv()
    out[0, other] = last_vector(theirs)

    pltpu.make_async_copy(left, left, l_send).wait()
    pltpu.make_async_copy(right, right, r_send).wait()
    pat_copy.wait_send()
    for i in range(4):
        final_copy(i).wait_send()
    for k in range(ITERS):
        for n, d in enumerate(shifts):
            pltpu.make_async_remote_copy(
                slots[k].at[HALO], slots[k].at[HALO - d],
                halo_send.at[k, n], halo_recv.at[k, n],
                device_id=at_sector(d), device_id_type=MESH,
            ).wait_send()
    for k in range(ROUNDS):
        exchange_wait(red_z, k, nz - 1, z_send)
        exchange_wait(red_y, k, 2 * NY - 1, y_send)


def on_device(nseg, nsec, psi, left, right, block, keep_l, keep_r, pattern, charge):
    here, size = left.shape[1], left.shape[3]
    count = 2 * nsec * size * size
    nz = nsec // NY
    pin = lambda x: pltpu.with_memory_space_constraint(x, pltpu.HBM)
    vmem = pl.BlockSpec(memory_space=pltpu.VMEM)
    hbm = pl.BlockSpec(memory_space=pltpu.HBM)
    square = (size, size)
    dma = pltpu.SemaphoreType.DMA
    halo = pltpu.VMEM((2 * HALO + 2, *square), BF16)
    terms = 2 * here
    return pl.pallas_call(
        functools.partial(kernel, nseg, nsec, here, size, count),
        out_shape=(
            jax.ShapeDtypeStruct(psi.shape, F32),
            jax.ShapeDtypeStruct((1, 2 * ITERS), F32),
        ),
        in_specs=[hbm] * 8,
        out_specs=(vmem, vmem),
        scratch_shapes=[
            pltpu.VMEM((terms, *square), BF16),
            pltpu.VMEM((terms, *square), BF16),
            halo, halo, halo, halo,
            pltpu.VMEM(square, F32),
            pltpu.VMEM(square, F32),
            *[pltpu.VMEM(square, F32)] * 8,
            pltpu.VMEM((4, *square), F32),
            pltpu.VMEM((4, *square), F32),
            pltpu.VMEM(square, F32),
            pltpu.VMEM(square, BF16),
            pltpu.VMEM((2, here), jnp.int32),
            pltpu.SMEM((2, 2, here), jnp.int32),
            pltpu.SMEM((1, 2), jnp.int32),
            pltpu.SMEM((1, 2), jnp.int32),
            pltpu.SMEM((terms,), jnp.int32),
            pltpu.SMEM((terms,), jnp.int32),
            pltpu.VMEM((ROUNDS, nz, 1, 128), F32),
            pltpu.VMEM((ROUNDS, 2 * NY, 1, 128), F32),
            pltpu.SemaphoreType.REGULAR, pltpu.SemaphoreType.REGULAR,
            dma((6,)), dma, dma, dma((terms,)), dma((terms,)),
            dma((ITERS, 4)), dma((ITERS, 4)),
            dma((ROUNDS,)), dma((ROUNDS,)),
            dma((ROUNDS,)), dma((ROUNDS,)),
            dma, dma, dma((4,)), dma((4,)),
        ],
        compiler_params=pltpu.CompilerParams(
            collective_id=0, has_side_effects=True, vmem_limit_bytes=48 << 20
        ),
    )(*map(pin, (psi, left, right, block, keep_l, keep_r, jnp.transpose(pattern, (0, 2, 1)), charge)))


def solution(mesh):
    placed = (
        P("seg", "sec", None, None),
        P("seg", "rep", "sec", None, None),
        P("seg", "rep", "sec", None, None),
        P("seg", "sec", None, None),
        P("seg", "sec"),
        P("seg", "sec"),
        P("seg", "rep", "sec"),
        P(),
    )
    return jax.shard_map(
        functools.partial(on_device, mesh.shape["seg"], mesh.shape["sec"]),
        mesh=mesh,
        in_specs=placed,
        out_specs=(P("seg", "sec", None, None), P("seg", None)),
        check_vma=False,
    )
```

```python
import functools

import jax
import jax.numpy as jnp
from jax import lax
from jax.experimental import pallas as pl
from jax.experimental.pallas import tpu as pltpu
from jax.sharding import PartitionSpec as P

ITERS = 4
NY = 4
HALO = 2
ROUNDS = 4
INITIAL = ROUNDS - 1
SUMS = 16
F32 = jnp.float32
BF16 = jnp.bfloat16
MESH = pl.DeviceIdType.MESH


def nt_dot(a, b):
    return lax.dot_general(a, b, (((1,), (1,)), ((), ())), preferred_element_type=F32)


def outward(n):
    return sorted(range(1, n), key=lambda i: -min(i, n - i))


def column_sums(x):
    total = jnp.sum(x, axis=0, keepdims=True)
    width = total.shape[1] // 2
    return total[:, :width] + total[:, width:]


def kernel(
    nseg, nsec, here, size, count,
    psi, left, right, block, keep_l, keep_r, pattern, charge,
    out, coeffs,
    lbuf, rbuf, vs0, vs1, vs2, vs3, acc, mask, v0, e1, e2, v1, u1, w1, hu1, hw1, mine, theirs,
    psi_v, blk_v, pat_v, pat_s, kl_s, kr_s, charge_s, index, red_z, red_y,
    near_sem, far_sem, load, l_send, r_send, l_recv, r_recv, halo_send, halo_recv,
    z_send, z_recv, y_send, y_recv, pat_send, pat_recv, fin_send, fin_recv,
):
    slots = (vs0, vs1, vs2, vs3)
    seg, sec, rep = lax.axis_index("seg"), lax.axis_index("sec"), lax.axis_index("rep")
    nz = nsec // NY
    z, y = sec // NY, sec % NY
    other = 1 - rep
    sector, sectors = 2 * sec + rep, 2 * nsec
    ahead, behind = (seg + 1) % nseg, (seg + nseg - 1) % nseg
    terms = 2 * here

    def at_sector(shift):
        s = (sector + sectors + shift) % sectors
        return (seg, s // 2, s % 2)

    sign = 2 * rep - 1
    shifts = (sign, 2 * sign, -2 * sign, -sign)
    z_peers = [(seg, ((z + i) % nz) * NY + y, rep) for i in outward(nz)]
    mine_y = 2 * y + rep
    y_peers = []
    for i in outward(2 * NY):
        p = (mine_y + i) % (2 * NY)
        y_peers.append((seg, z * NY + p // 2, p % 2))

    def at_yz(dy, dz, r):
        return (seg, ((z + nz + dz) % nz) * NY + (y + NY + dy) % NY, r)

    partners = [(a, sec, jnp.int32(r)) for a in (ahead, behind) for r in range(2)]
    partners += [at_yz(0, d, rep) for d in (-1, 1)]
    partners += [at_yz(d, 0, jnp.int32(r)) for d in (-1, 1) for r in range(2)]
    partners += [(seg, sec, other)]
    barrier = pltpu.get_barrier_semaphore()
    for p in partners:
        pl.semaphore_signal(barrier, inc=1, device_id=p, device_id_type=MESH)
    loads = [
        pltpu.make_async_copy(a, b, load.at[i])
        for i, (a, b) in enumerate([
            (psi.at[0, rep], psi_v), (block.at[0, rep], blk_v), (pattern.at[0], pat_s.at[rep]),
            (keep_l, kl_s), (keep_r, kr_s), (charge, charge_s),
        ])
    ]
    for c in loads:
        c.start()
    pl.semaphore_wait(barrier, len(partners))

    def left_copy(t, r):
        w = rep * here + t
        return pltpu.make_async_remote_copy(
            left.at[0, t, r], lbuf.at[w], l_send, l_recv.at[w],
            device_id=(ahead, sec, r), device_id_type=MESH,
        )

    def right_copy(t, r):
        w = rep * here + t
        return pltpu.make_async_remote_copy(
            right.at[0, t, r], rbuf.at[w], r_send, r_recv.at[w],
            device_id=(behind, sec, r), device_id_type=MESH,
        )

    for i in range(2):
        @pl.loop(0, here)
        def _(t):
            left_copy(t, (sec + i) % 2).start()
            right_copy(t, (sec + i) % 2).start()

    def start_halo(k):
        for n, d in enumerate(shifts):
            pltpu.make_async_remote_copy(
                slots[k].at[HALO], slots[k].at[HALO - d],
                halo_send.at[k, n], halo_recv.at[k, n],
                device_id=at_sector(d), device_id_type=MESH,
            ).start()

    def wait_halo(k):
        for n, d in enumerate(shifts):
            pltpu.make_async_remote_copy(
                slots[k].at[HALO], slots[k].at[HALO - d],
                halo_send.at[k, n], halo_recv.at[k, n],
                device_id=at_sector(d), device_id_type=MESH,
            ).wait_recv()

    def exchange_start(buf, k, mine, peers, send, recv):
        for p in peers:
            pltpu.make_async_remote_copy(
                buf.at[k, mine], buf.at[k, mine], send.at[k], recv.at[k],
                device_id=p, device_id_type=MESH,
            ).start()

    def exchange_wait(buf, k, n, sem):
        some = buf.at[k, pl.ds(0, n)]
        pltpu.make_async_copy(some, some, sem.at[k]).wait()

    def total_of(buf, k, n):
        total = buf[k, 0]
        for i in range(1, n):
            total = total + buf[k, i]
        return total

    lanes = lax.broadcasted_iota(jnp.int32, (SUMS, 128), 1)
    diagonal = lanes == lax.broadcasted_iota(jnp.int32, (SUMS, 128), 0)

    def reduce_first(k, rows):
        rows = rows + [jnp.zeros((SUMS - len(rows), 128), F32)]
        sums = jnp.sum(jnp.concatenate(rows, axis=0), axis=1, keepdims=True)
        red_y[k, mine_y] = jnp.sum(jnp.where(diagonal, sums, 0.0), axis=0, keepdims=True)
        exchange_start(red_y, k, mine_y, y_peers, y_send, y_recv)

    def reduce_second(k):
        exchange_wait(red_y, k, 2 * NY - 1, y_recv)
        red_z[k, z] = total_of(red_y, k, 2 * NY)
        exchange_start(red_z, k, z, z_peers, z_send, z_recv)

    def reduce_last(k):
        exchange_wait(red_z, k, nz - 1, z_recv)
        total = jnp.where(diagonal, total_of(red_z, k, nz), 0.0)
        return jnp.sum(total, axis=1, keepdims=True) * (1.0 / count)

    near = [at_yz(0, d, rep) for d in (-1, 1)] + [at_yz(d, 0, rep) for d in (-1, 1)]
    for p in near:
        pl.semaphore_signal(near_sem, inc=1, device_id=p, device_id_type=MESH)
    pl.semaphore_wait(near_sem, len(near))
    far = [at_yz(0, d, rep) for d in (-2, 2)]
    for p in far:
        pl.semaphore_signal(far_sem, inc=1, device_id=p, device_id_type=MESH)
    pl.semaphore_wait(far_sem, len(far))

    pat_copy = pltpu.make_async_remote_copy(
        pattern.at[0], pat_v, pat_send, pat_recv, device_id=(seg, sec, other), device_id_type=MESH
    )
    pat_copy.start()
    for c in loads:
        c.wait()

    rows = lax.broadcasted_iota(jnp.int32, (size, size), 0)
    cols = lax.broadcasted_iota(jnp.int32, (size, size), 1)
    inside = (rows < kl_s[0, rep]) & (cols < kr_s[0, rep])
    mask[...] = inside.astype(F32)
    start = mask[...] * psi_v[...]
    v0[...] = start
    reduce_first(INITIAL, [column_sums(start * start)])

    pat_copy.wait_recv()
    move = pltpu.make_async_copy(pat_v, pat_s.at[other], load.at[0])
    move.start()
    move.wait()

    for k in range(ITERS):
        slots[k][2 * HALO + 1] = jnp.zeros((size, size), BF16)

    @pl.loop(0, terms)
    def _(w):
        c = charge_s[w]
        to = sector + c
        index[w] = jnp.where((to >= 0) & (to < sectors), c + HALO, 2 * HALO + 1)

    reduce_second(INITIAL)
    scale = reduce_last(INITIAL)[0:1]
    v0[...] = v0[...] * lax.rsqrt(scale + 1e-06)
    slots[0][HALO] = v0[...].astype(BF16)
    start_halo(0)

    def apply_local(k):
        half = size // 2

        @pl.loop(0, 2)
        def _(i):
            some = pl.ds(pl.multiple_of(i * half, half), half)
            first = jnp.dot(blk_v[some, :], slots[k][HALO], preferred_element_type=F32)
            acc[some, :] = first + nt_dot(slots[k][HALO, some, :], blk_v[...])

    def term(k, q, t):
        w = q * here + t
        moved = slots[k][index[w]]
        inner = jnp.dot(lbuf[w], moved, preferred_element_type=F32)
        inner = (inner * pat_s[q, rep, t].astype(F32)).astype(BF16)
        return nt_dot(inner, rbuf[w])

    def env_wait(w):
        pltpu.make_async_remote_copy(
            left.at[0, 0, 0], lbuf.at[w], l_send, l_recv.at[w],
            device_id=(ahead, sec, rep), device_id_type=MESH,
        ).wait_recv()
        pltpu.make_async_remote_copy(
            right.at[0, 0, 0], rbuf.at[w], r_send, r_recv.at[w],
            device_id=(behind, sec, rep), device_id_type=MESH,
        ).wait_recv()

    def apply_rest(k):
        wait_halo(k)
        total = acc[...]
        for t in range(here):
            for q in range(2):
                total = total + term(k, q, t)
        return total

    def offer(k, x):
        slots[k][HALO] = x.astype(BF16)
        start_halo(k)

    def dot(a, b):
        return column_sums(a * b)

    def coefficients(means, vu, vw, vv, ww):
        alpha = means[vu : vu + 1]
        rest = means[ww : ww + 1] - 2.0 * alpha * means[vw : vw + 1] + alpha * alpha * means[vv : vv + 1]
        return alpha, jnp.sqrt(jnp.maximum(rest, 0.0) + 1e-06)

    apply_local(0)
    wait_halo(0)

    @pl.loop(0, here)
    def _(t):
        env_wait(t)
        env_wait(here + t)
        acc[...] += term(0, 0, t) + term(0, 1, t)

    offer(1, mask[...] * acc[...])
    e1[...] = mask[...] * acc[...]
    reduce_first(0, [dot(v0[...], e1[...]), dot(e1[...], e1[...]), dot(v0[...], v0[...])])
    apply_local(1)
    total = apply_rest(1)

    offer(2, mask[...] * total)
    e2[...] = mask[...] * total
    reduce_second(0)
    apply_local(2)
    alpha0, beta0 = coefficients(reduce_last(0), 0, 0, 2, 1)
    inverse0 = 1.0 / beta0
    v1[...] = (e1[...] - alpha0 * v0[...]) * inverse0
    u1[...] = (e2[...] - alpha0 * e1[...]) * inverse0
    w1[...] = u1[...] - beta0 * v0[...]
    reduce_first(1, [dot(v1[...], u1[...]), dot(v1[...], w1[...]), dot(v1[...], v1[...]), dot(w1[...], w1[...])])
    total = apply_rest(2)

    image = (mask[...] * total - alpha0 * e2[...]) * inverse0
    offer(3, image - beta0 * e1[...])
    hu1[...] = image
    hw1[...] = image - beta0 * e1[...]
    reduce_second(1)
    apply_local(3)
    alpha1, beta1 = coefficients(reduce_last(1), 0, 1, 2, 3)
    inverse1 = 1.0 / beta1
    mine[0] = (w1[...] - alpha1 * v1[...]) * inverse1
    mine[1] = (hw1[...] - alpha1 * u1[...]) * inverse1
    mine[2] = mine[1] - beta1 * v1[...]

    def final_copy(i):
        return pltpu.make_async_remote_copy(
            mine.at[i], theirs.at[i], fin_send.at[i], fin_recv.at[i],
            device_id=(seg, sec, other), device_id_type=MESH,
        )

    for i in range(3):
        final_copy(i).start()
    hu1[...] = alpha1 * hu1[...] + beta1 * beta1 * u1[...]
    v2, u2, w2 = mine[0], mine[1], mine[2]
    early = [dot(v2, u2), dot(v2, w2), dot(v2, v2), dot(w2, w2), dot(w2, u2), dot(u2, u2)]
    total = apply_rest(3)

    mine[3] = (mask[...] * total - hu1[...]) * inverse1
    h, v2, u2, w2 = mine[3], mine[0], mine[1], mine[2]
    reduce_first(2, early + [dot(w2, h), dot(v2, h), dot(h, h), dot(u2, h)])
    final_copy(3).start()
    reduce_second(2)
    means = reduce_last(2)
    vu, vw, vv, ww, wu, uu, wh, vh, hh, uh = (means[i : i + 1] for i in range(10))
    alpha2, beta2 = coefficients(means, 0, 1, 2, 3)
    square2 = beta2 * beta2
    inverse2 = 1.0 / square2
    alpha3 = (wh - alpha2 * (wu + vh) + alpha2 * alpha2 * vu) * inverse2
    ww3 = (
        hh + alpha2 * alpha2 * uu + square2 * square2 * vv
        - 2.0 * (alpha2 * uh + square2 * vh) + 2.0 * alpha2 * square2 * vu
    ) * inverse2
    vv3 = (ww - 2.0 * alpha2 * vw + alpha2 * alpha2 * vv) * inverse2
    vw3 = alpha3 - vw + alpha2 * vv
    rest = ww3 - 2.0 * alpha3 * vw3 + alpha3 * alpha3 * vv3
    beta3 = jnp.sqrt(jnp.maximum(rest, 0.0) + 1e-06)
    coeffs[...] = jnp.concatenate([alpha0, alpha1, alpha2, alpha3, beta0, beta1, beta2, beta3], axis=1)
    outer = 1.0 / (beta2 * beta3)
    along_v = (alpha3 * alpha2 - square2) * outer
    along_u, along_w = -alpha2 * outer, -alpha3 * outer

    def last_vector(parts):
        return outer * parts[3] + along_u * parts[1] + along_w * parts[2] + along_v * parts[0]

    out[0, rep] = last_vector(mine)
    for i in range(4):
        final_copy(i).wait_recv()
    out[0, other] = last_vector(theirs)

    pltpu.make_async_copy(left, left, l_send).wait()
    pltpu.make_async_copy(right, right, r_send).wait()
    pat_copy.wait_send()
    for i in range(4):
        final_copy(i).wait_send()
    for k in range(ITERS):
        for n, d in enumerate(shifts):
            pltpu.make_async_remote_copy(
                slots[k].at[HALO], slots[k].at[HALO - d],
                halo_send.at[k, n], halo_recv.at[k, n],
                device_id=at_sector(d), device_id_type=MESH,
            ).wait_send()
    for k in range(ROUNDS):
        exchange_wait(red_z, k, nz - 1, z_send)
        exchange_wait(red_y, k, 2 * NY - 1, y_send)


def on_device(nseg, nsec, psi, left, right, block, keep_l, keep_r, pattern, charge):
    here, size = left.shape[1], left.shape[3]
    count = 2 * nsec * size * size
    nz = nsec // NY
    pin = lambda x: pltpu.with_memory_space_constraint(x, pltpu.HBM)
    vmem = pl.BlockSpec(memory_space=pltpu.VMEM)
    hbm = pl.BlockSpec(memory_space=pltpu.HBM)
    square = (size, size)
    dma = pltpu.SemaphoreType.DMA
    halo = pltpu.VMEM((2 * HALO + 2, *square), BF16)
    terms = 2 * here
    return pl.pallas_call(
        functools.partial(kernel, nseg, nsec, here, size, count),
        out_shape=(
            jax.ShapeDtypeStruct(psi.shape, F32),
            jax.ShapeDtypeStruct((1, 2 * ITERS), F32),
        ),
        in_specs=[hbm] * 8,
        out_specs=(vmem, vmem),
        scratch_shapes=[
            pltpu.VMEM((terms, *square), BF16),
            pltpu.VMEM((terms, *square), BF16),
            halo, halo, halo, halo,
            pltpu.VMEM(square, F32),
            pltpu.VMEM(square, F32),
            *[pltpu.VMEM(square, F32)] * 8,
            pltpu.VMEM((4, *square), F32),
            pltpu.VMEM((4, *square), F32),
            pltpu.VMEM(square, F32),
            pltpu.VMEM(square, BF16),
            pltpu.VMEM((2, here), jnp.int32),
            pltpu.SMEM((2, 2, here), jnp.int32),
            pltpu.SMEM((1, 2), jnp.int32),
            pltpu.SMEM((1, 2), jnp.int32),
            pltpu.SMEM((terms,), jnp.int32),
            pltpu.SMEM((terms,), jnp.int32),
            pltpu.VMEM((ROUNDS, nz, 1, 128), F32),
            pltpu.VMEM((ROUNDS, 2 * NY, 1, 128), F32),
            pltpu.SemaphoreType.REGULAR, pltpu.SemaphoreType.REGULAR,
            dma((6,)), dma, dma, dma((terms,)), dma((terms,)),
            dma((ITERS, 4)), dma((ITERS, 4)),
            dma((ROUNDS,)), dma((ROUNDS,)),
            dma((ROUNDS,)), dma((ROUNDS,)),
            dma, dma, dma((4,)), dma((4,)),
        ],
        compiler_params=pltpu.CompilerParams(
            collective_id=0, has_side_effects=True, vmem_limit_bytes=48 << 20
        ),
    )(*map(pin, (psi, left, right, block, keep_l, keep_r, jnp.transpose(pattern, (0, 2, 1)), charge)))


def solution(mesh):
    placed = (
        P("seg", "sec", None, None),
        P("seg", "rep", "sec", None, None),
        P("seg", "rep", "sec", None, None),
        P("seg", "sec", None, None),
        P("seg", "sec"),
        P("seg", "sec"),
        P("seg", "rep", "sec"),
        P(),
    )
    return jax.shard_map(
        functools.partial(on_device, mesh.shape["seg"], mesh.shape["sec"]),
        mesh=mesh,
        in_specs=placed,
        out_specs=(P("seg", "sec", None, None), P("seg", None)),
        check_vma=False,
    )
```

```python
import functools

import jax
import jax.numpy as jnp
from jax import lax
from jax.experimental import pallas as pl
from jax.experimental.pallas import tpu as pltpu
from jax.sharding import PartitionSpec as P

ITERS = 4
NY = 4
HALO = 2
ROUNDS = 4
INITIAL = ROUNDS - 1
SUMS = 16
F32 = jnp.float32
BF16 = jnp.bfloat16
MESH = pl.DeviceIdType.MESH


def nt_dot(a, b):
    return lax.dot_general(a, b, (((1,), (1,)), ((), ())), preferred_element_type=F32)


def outward(n):
    return sorted(range(1, n), key=lambda i: -min(i, n - i))


def column_sums(x):
    total = jnp.sum(x, axis=0, keepdims=True)
    width = total.shape[1] // 2
    return total[:, :width] + total[:, width:]


def kernel(
    nseg, nsec, here, size, count,
    psi, left, right, block, keep_l, keep_r, pattern, charge,
    out, coeffs,
    lbuf, rbuf, vs0, vs1, vs2, vs3, acc, mask, v0, e1, e2, v1, u1, w1, hu1, hw1, mine, theirs,
    psi_v, blk_v, pat_v, pat_s, kl_s, kr_s, charge_s, index, red_z, red_y,
    near_sem, far_sem, load, l_send, r_send, l_recv, r_recv, halo_send, halo_recv,
    z_send, z_recv, y_send, y_recv, pat_send, pat_recv, fin_send, fin_recv,
):
    slots = (vs0, vs1, vs2, vs3)
    seg, sec, rep = lax.axis_index("seg"), lax.axis_index("sec"), lax.axis_index("rep")
    nz = nsec // NY
    z, y = sec // NY, sec % NY
    other = 1 - rep
    sector, sectors = 2 * sec + rep, 2 * nsec
    ahead, behind = (seg + 1) % nseg, (seg + nseg - 1) % nseg
    terms = 2 * here

    def at_sector(shift):
        s = (sector + sectors + shift) % sectors
        return (seg, s // 2, s % 2)

    sign = 2 * rep - 1
    shifts = (sign, 2 * sign, -2 * sign, -sign)
    z_peers = [(seg, ((z + i) % nz) * NY + y, rep) for i in outward(nz)]
    mine_y = 2 * y + rep
    y_peers = []
    for i in outward(2 * NY):
        p = (mine_y + i) % (2 * NY)
        y_peers.append((seg, z * NY + p // 2, p % 2))

    def at_yz(dy, dz, r):
        return (seg, ((z + nz + dz) % nz) * NY + (y + NY + dy) % NY, r)

    partners = [(a, sec, jnp.int32(r)) for a in (ahead, behind) for r in range(2)]
    partners += [at_yz(0, d, rep) for d in (-1, 1)]
    partners += [at_yz(d, 0, jnp.int32(r)) for d in (-1, 1) for r in range(2)]
    partners += [(seg, sec, other)]
    barrier = pltpu.get_barrier_semaphore()
    for p in partners:
        pl.semaphore_signal(barrier, inc=1, device_id=p, device_id_type=MESH)
    loads = [
        pltpu.make_async_copy(a, b, load.at[i])
        for i, (a, b) in enumerate([
            (psi.at[0, rep], psi_v), (block.at[0, rep], blk_v), (pattern.at[0], pat_s.at[rep]),
            (keep_l, kl_s), (keep_r, kr_s), (charge, charge_s),
        ])
    ]
    for c in loads:
        c.start()
    pl.semaphore_wait(barrier, len(partners))

    def left_copy(t, r):
        w = rep * here + t
        return pltpu.make_async_remote_copy(
            left.at[0, t, r], lbuf.at[w], l_send, l_recv.at[w],
            device_id=(ahead, sec, r), device_id_type=MESH,
        )

    def right_copy(t, r):
        w = rep * here + t
        return pltpu.make_async_remote_copy(
            right.at[0, t, r], rbuf.at[w], r_send, r_recv.at[w],
            device_id=(behind, sec, r), device_id_type=MESH,
        )

    for i in range(2):
        @pl.loop(0, here)
        def _(t):
            left_copy(t, (sec + i) % 2).start()
            right_copy(t, (sec + i) % 2).start()

    def start_halo(k):
        for n, d in enumerate(shifts):
            pltpu.make_async_remote_copy(
                slots[k].at[HALO], slots[k].at[HALO - d],
                halo_send.at[k, n], halo_recv.at[k, n],
                device_id=at_sector(d), device_id_type=MESH,
            ).start()

    def wait_halo(k):
        for n, d in enumerate(shifts):
            pltpu.make_async_remote_copy(
                slots[k].at[HALO], slots[k].at[HALO - d],
                halo_send.at[k, n], halo_recv.at[k, n],
                device_id=at_sector(d), device_id_type=MESH,
            ).wait_recv()

    def exchange_start(buf, k, mine, peers, send, recv):
        for p in peers:
            pltpu.make_async_remote_copy(
                buf.at[k, mine], buf.at[k, mine], send.at[k], recv.at[k],
                device_id=p, device_id_type=MESH,
            ).start()

    def exchange_wait(buf, k, n, sem):
        some = buf.at[k, pl.ds(0, n)]
        pltpu.make_async_copy(some, some, sem.at[k]).wait()

    def total_of(buf, k, n):
        total = buf[k, 0]
        for i in range(1, n):
            total = total + buf[k, i]
        return total

    lanes = lax.broadcasted_iota(jnp.int32, (SUMS, 128), 1)
    diagonal = lanes == lax.broadcasted_iota(jnp.int32, (SUMS, 128), 0)

    def reduce_first(k, rows):
        rows = rows + [jnp.zeros((SUMS - len(rows), 128), F32)]
        sums = jnp.sum(jnp.concatenate(rows, axis=0), axis=1, keepdims=True)
        red_y[k, mine_y] = jnp.sum(jnp.where(diagonal, sums, 0.0), axis=0, keepdims=True)
        exchange_start(red_y, k, mine_y, y_peers, y_send, y_recv)

    def reduce_second(k):
        exchange_wait(red_y, k, 2 * NY - 1, y_recv)
        red_z[k, z] = total_of(red_y, k, 2 * NY)
        exchange_start(red_z, k, z, z_peers, z_send, z_recv)

    def reduce_last(k):
        exchange_wait(red_z, k, nz - 1, z_recv)
        total = jnp.where(diagonal, total_of(red_z, k, nz), 0.0)
        return jnp.sum(total, axis=1, keepdims=True) * (1.0 / count)

    near = [at_yz(0, d, rep) for d in (-1, 1)] + [at_yz(d, 0, rep) for d in (-1, 1)]
    for p in near:
        pl.semaphore_signal(near_sem, inc=1, device_id=p, device_id_type=MESH)
    pl.semaphore_wait(near_sem, len(near))
    far = [at_yz(0, d, rep) for d in (-2, 2)]
    for p in far:
        pl.semaphore_signal(far_sem, inc=1, device_id=p, device_id_type=MESH)
    pl.semaphore_wait(far_sem, len(far))

    pat_copy = pltpu.make_async_remote_copy(
        pattern.at[0], pat_v, pat_send, pat_recv, device_id=(seg, sec, other), device_id_type=MESH
    )
    pat_copy.start()
    for c in loads:
        c.wait()

    rows = lax.broadcasted_iota(jnp.int32, (size, size), 0)
    cols = lax.broadcasted_iota(jnp.int32, (size, size), 1)
    inside = (rows < kl_s[0, rep]) & (cols < kr_s[0, rep])
    mask[...] = inside.astype(F32)
    start = mask[...] * psi_v[...]
    v0[...] = start
    reduce_first(INITIAL, [column_sums(start * start)])

    pat_copy.wait_recv()
    move = pltpu.make_async_copy(pat_v, pat_s.at[other], load.at[0])
    move.start()
    move.wait()

    for k in range(ITERS):
        slots[k][2 * HALO + 1] = jnp.zeros((size, size), BF16)

    @pl.loop(0, terms)
    def _(w):
        c = charge_s[w]
        to = sector + c
        index[w] = jnp.where((to >= 0) & (to < sectors), c + HALO, 2 * HALO + 1)

    reduce_second(INITIAL)
    scale = reduce_last(INITIAL)[0:1]
    v0[...] = v0[...] * lax.rsqrt(scale + 1e-06)
    slots[0][HALO] = v0[...].astype(BF16)
    start_halo(0)

    def apply_local(k):
        half = size // 2

        @pl.loop(0, 2)
        def _(i):
            some = pl.ds(pl.multiple_of(i * half, half), half)
            first = jnp.dot(blk_v[some, :], slots[k][HALO], preferred_element_type=F32)
            acc[some, :] = first + nt_dot(slots[k][HALO, some, :], blk_v[...])

    def term(k, q, t):
        w = q * here + t
        moved = slots[k][index[w]]
        inner = jnp.dot(lbuf[w], moved, preferred_element_type=F32)
        inner = (inner * pat_s[q, rep, t].astype(F32)).astype(BF16)
        return nt_dot(inner, rbuf[w])

    def env_wait(w):
        pltpu.make_async_remote_copy(
            left.at[0, 0, 0], lbuf.at[w], l_send, l_recv.at[w],
            device_id=(ahead, sec, rep), device_id_type=MESH,
        ).wait_recv()
        pltpu.make_async_remote_copy(
            right.at[0, 0, 0], rbuf.at[w], r_send, r_recv.at[w],
            device_id=(behind, sec, rep), device_id_type=MESH,
        ).wait_recv()

    def apply_rest(k):
        wait_halo(k)
        total = acc[...]
        for t in range(here):
            for q in range(2):
                total = total + term(k, q, t)
        return total

    def offer(k, x):
        slots[k][HALO] = x.astype(BF16)
        start_halo(k)

    def dot(a, b):
        return column_sums(a * b)

    def coefficients(means, vu, vw, vv, ww):
        alpha = means[vu : vu + 1]
        rest = means[ww : ww + 1] - 2.0 * alpha * means[vw : vw + 1] + alpha * alpha * means[vv : vv + 1]
        return alpha, jnp.sqrt(jnp.maximum(rest, 0.0) + 1e-06)

    def following(alpha, square, vu, vw, vv, ww, wu, uu, wh, vh, hh, uh):
        inverse = 1.0 / square
        alpha_next = (wh - alpha * (wu + vh) + alpha * alpha * vu) * inverse
        ww_next = (
            hh + alpha * alpha * uu + square * square * vv
            - 2.0 * (alpha * uh + square * vh) + 2.0 * alpha * square * vu
        ) * inverse
        vv_next = (ww - 2.0 * alpha * vw + alpha * alpha * vv) * inverse
        vw_next = alpha_next - vw + alpha * vv
        rest = ww_next - 2.0 * alpha_next * vw_next + alpha_next * alpha_next * vv_next
        return alpha_next, jnp.sqrt(jnp.maximum(rest, 0.0) + 1e-06)

    apply_local(0)
    wait_halo(0)

    @pl.loop(0, here)
    def _(t):
        env_wait(t)
        env_wait(here + t)
        acc[...] += term(0, 0, t) + term(0, 1, t)

    offer(1, mask[...] * acc[...])
    e1[...] = mask[...] * acc[...]
    reduce_first(0, [dot(v0[...], e1[...]), dot(e1[...], e1[...]), dot(v0[...], v0[...])])
    apply_local(1)
    total = apply_rest(1)

    offer(2, mask[...] * total)
    e2[...] = mask[...] * total
    reduce_second(0)
    reduce_first(1, [dot(e1[...], e2[...]), dot(v0[...], e2[...]), dot(e2[...], e2[...])])
    apply_local(2)
    total = apply_rest(2)
    means0 = reduce_last(0)
    alpha0, beta0 = coefficients(means0, 0, 0, 2, 1)
    inverse0 = 1.0 / beta0

    image = (mask[...] * total - alpha0 * e2[...]) * inverse0
    offer(3, image - beta0 * e1[...])
    hu1[...] = image
    hw1[...] = image - beta0 * e1[...]
    reduce_second(1)
    apply_local(3)
    v1[...] = (e1[...] - alpha0 * v0[...]) * inverse0
    u1[...] = (e2[...] - alpha0 * e1[...]) * inverse0
    w1[...] = u1[...] - beta0 * v0[...]
    means1 = reduce_last(1)
    vu0, uu0, vv0 = (means0[i : i + 1] for i in range(3))
    uh0, vh0, hh0 = (means1[i : i + 1] for i in range(3))
    alpha1, beta1 = following(alpha0, beta0 * beta0, vu0, vu0, vv0, uu0, uu0, uu0, uh0, vh0, hh0, uh0)
    inverse1 = 1.0 / beta1
    mine[0] = (w1[...] - alpha1 * v1[...]) * inverse1
    mine[1] = (hw1[...] - alpha1 * u1[...]) * inverse1
    mine[2] = mine[1] - beta1 * v1[...]

    def final_copy(i):
        return pltpu.make_async_remote_copy(
            mine.at[i], theirs.at[i], fin_send.at[i], fin_recv.at[i],
            device_id=(seg, sec, other), device_id_type=MESH,
        )

    for i in range(3):
        final_copy(i).start()
    hu1[...] = alpha1 * hu1[...] + beta1 * beta1 * u1[...]
    v2, u2, w2 = mine[0], mine[1], mine[2]
    early = [dot(v2, u2), dot(v2, w2), dot(v2, v2), dot(w2, w2), dot(w2, u2), dot(u2, u2)]
    total = apply_rest(3)

    mine[3] = (mask[...] * total - hu1[...]) * inverse1
    h, v2, u2, w2 = mine[3], mine[0], mine[1], mine[2]
    reduce_first(2, early + [dot(w2, h), dot(v2, h), dot(h, h), dot(u2, h)])
    final_copy(3).start()
    reduce_second(2)
    pltpu.make_async_copy(left, left, l_send).wait()
    pltpu.make_async_copy(right, right, r_send).wait()
    pat_copy.wait_send()
    for k in range(ITERS):
        for n, d in enumerate(shifts):
            pltpu.make_async_remote_copy(
                slots[k].at[HALO], slots[k].at[HALO - d],
                halo_send.at[k, n], halo_recv.at[k, n],
                device_id=at_sector(d), device_id_type=MESH,
            ).wait_send()
    for k in (0, 1, INITIAL):
        exchange_wait(red_z, k, nz - 1, z_send)
        exchange_wait(red_y, k, 2 * NY - 1, y_send)
    for i in range(4):
        final_copy(i).wait()
    means = reduce_last(2)
    vu, vw, vv, ww, wu, uu, wh, vh, hh, uh = (means[i : i + 1] for i in range(10))
    alpha2, beta2 = coefficients(means, 0, 1, 2, 3)
    square2 = beta2 * beta2
    alpha3, beta3 = following(alpha2, square2, vu, vw, vv, ww, wu, uu, wh, vh, hh, uh)
    coeffs[...] = jnp.concatenate([alpha0, alpha1, alpha2, alpha3, beta0, beta1, beta2, beta3], axis=1)
    outer = 1.0 / (beta2 * beta3)
    along_v = (alpha3 * alpha2 - square2) * outer
    along_u, along_w = -alpha2 * outer, -alpha3 * outer

    def last_vector(parts):
        return outer * parts[3] + along_u * parts[1] + along_w * parts[2] + along_v * parts[0]

    out[0, rep] = last_vector(mine)
    out[0, other] = last_vector(theirs)

    exchange_wait(red_z, 2, nz - 1, z_send)
    exchange_wait(red_y, 2, 2 * NY - 1, y_send)


def on_device(nseg, nsec, psi, left, right, block, keep_l, keep_r, pattern, charge):
    here, size = left.shape[1], left.shape[3]
    count = 2 * nsec * size * size
    nz = nsec // NY
    pin = lambda x: pltpu.with_memory_space_constraint(x, pltpu.HBM)
    vmem = pl.BlockSpec(memory_space=pltpu.VMEM)
    hbm = pl.BlockSpec(memory_space=pltpu.HBM)
    square = (size, size)
    dma = pltpu.SemaphoreType.DMA
    halo = pltpu.VMEM((2 * HALO + 2, *square), BF16)
    terms = 2 * here
    return pl.pallas_call(
        functools.partial(kernel, nseg, nsec, here, size, count),
        out_shape=(
            jax.ShapeDtypeStruct(psi.shape, F32),
            jax.ShapeDtypeStruct((1, 2 * ITERS), F32),
        ),
        in_specs=[hbm] * 8,
        out_specs=(vmem, vmem),
        scratch_shapes=[
            pltpu.VMEM((terms, *square), BF16),
            pltpu.VMEM((terms, *square), BF16),
            halo, halo, halo, halo,
            pltpu.VMEM(square, F32),
            pltpu.VMEM(square, F32),
            *[pltpu.VMEM(square, F32)] * 8,
            pltpu.VMEM((4, *square), F32),
            pltpu.VMEM((4, *square), F32),
            pltpu.VMEM(square, F32),
            pltpu.VMEM(square, BF16),
            pltpu.VMEM((2, here), jnp.int32),
            pltpu.SMEM((2, 2, here), jnp.int32),
            pltpu.SMEM((1, 2), jnp.int32),
            pltpu.SMEM((1, 2), jnp.int32),
            pltpu.SMEM((terms,), jnp.int32),
            pltpu.SMEM((terms,), jnp.int32),
            pltpu.VMEM((ROUNDS, nz, 1, 128), F32),
            pltpu.VMEM((ROUNDS, 2 * NY, 1, 128), F32),
            pltpu.SemaphoreType.REGULAR, pltpu.SemaphoreType.REGULAR,
            dma((6,)), dma, dma, dma((terms,)), dma((terms,)),
            dma((ITERS, 4)), dma((ITERS, 4)),
            dma((ROUNDS,)), dma((ROUNDS,)),
            dma((ROUNDS,)), dma((ROUNDS,)),
            dma, dma, dma((4,)), dma((4,)),
        ],
        compiler_params=pltpu.CompilerParams(
            collective_id=0, has_side_effects=True, vmem_limit_bytes=48 << 20
        ),
    )(*map(pin, (psi, left, right, block, keep_l, keep_r, jnp.transpose(pattern, (0, 2, 1)), charge)))


def solution(mesh):
    placed = (
        P("seg", "sec", None, None),
        P("seg", "rep", "sec", None, None),
        P("seg", "rep", "sec", None, None),
        P("seg", "sec", None, None),
        P("seg", "sec"),
        P("seg", "sec"),
        P("seg", "rep", "sec"),
        P(),
    )
    return jax.shard_map(
        functools.partial(on_device, mesh.shape["seg"], mesh.shape["sec"]),
        mesh=mesh,
        in_specs=placed,
        out_specs=(P("seg", "sec", None, None), P("seg", None)),
        check_vma=False,
    )
```

```python
import functools

import jax
import jax.numpy as jnp
from jax import lax
from jax.experimental import pallas as pl
from jax.experimental.pallas import tpu as pltpu
from jax.sharding import PartitionSpec as P

ITERS = 4
NY = 4
HALO = 2
ROUNDS = 4
INITIAL = ROUNDS - 1
SUMS = 16
F32 = jnp.float32
BF16 = jnp.bfloat16
MESH = pl.DeviceIdType.MESH


def nt_dot(a, b):
    return lax.dot_general(a, b, (((1,), (1,)), ((), ())), preferred_element_type=F32)


def outward(n):
    return sorted(range(1, n), key=lambda i: -min(i, n - i))


def column_sums(x):
    total = jnp.sum(x, axis=0, keepdims=True)
    width = total.shape[1] // 2
    return total[:, :width] + total[:, width:]


def kernel(
    nseg, nsec, here, size, count,
    psi, left, right, block, keep_l, keep_r, pattern, charge,
    out, coeffs,
    lbuf, rbuf, vs0, vs1, vs2, vs3, acc, mask, v0, e1, e2, v1, u1, w1, hu1, hw1, mine, theirs,
    psi_v, blk_v, pat_v, pat_s, kl_s, kr_s, charge_s, index, red_z, red_y,
    near_sem, far_sem, load, l_send, r_send, l_recv, r_recv, halo_send, halo_recv,
    z_send, z_recv, y_send, y_recv, pat_send, pat_recv, fin_send, fin_recv,
):
    slots = (vs0, vs1, vs2, vs3)
    seg, sec, rep = lax.axis_index("seg"), lax.axis_index("sec"), lax.axis_index("rep")
    nz = nsec // NY
    z, y = sec // NY, sec % NY
    other = 1 - rep
    sector, sectors = 2 * sec + rep, 2 * nsec
    ahead, behind = (seg + 1) % nseg, (seg + nseg - 1) % nseg
    terms = 2 * here

    def at_sector(shift):
        s = (sector + sectors + shift) % sectors
        return (seg, s // 2, s % 2)

    sign = 2 * rep - 1
    shifts = (sign, 2 * sign, -2 * sign, -sign)
    z_peers = [(seg, ((z + i) % nz) * NY + y, rep) for i in outward(nz)]
    mine_y = 2 * y + rep
    y_peers = []
    for i in outward(2 * NY):
        p = (mine_y + i) % (2 * NY)
        y_peers.append((seg, z * NY + p // 2, p % 2))

    def at_yz(dy, dz, r):
        return (seg, ((z + nz + dz) % nz) * NY + (y + NY + dy) % NY, r)

    partners = [(a, sec, jnp.int32(r)) for a in (ahead, behind) for r in range(2)]
    partners += [at_yz(0, d, rep) for d in (-1, 1)]
    partners += [at_yz(d, 0, jnp.int32(r)) for d in (-1, 1) for r in range(2)]
    partners += [(seg, sec, other)]
    barrier = pltpu.get_barrier_semaphore()
    for p in partners:
        pl.semaphore_signal(barrier, inc=1, device_id=p, device_id_type=MESH)
    loads = [
        pltpu.make_async_copy(a, b, load.at[i])
        for i, (a, b) in enumerate([
            (psi.at[0, rep], psi_v), (block.at[0, rep], blk_v), (pattern.at[0], pat_s.at[rep]),
            (keep_l, kl_s), (keep_r, kr_s), (charge, charge_s),
        ])
    ]
    for c in loads:
        c.start()
    pl.semaphore_wait(barrier, len(partners))

    def left_copy(t, r):
        w = rep * here + t
        return pltpu.make_async_remote_copy(
            left.at[0, t, r], lbuf.at[w], l_send, l_recv.at[w],
            device_id=(ahead, sec, r), device_id_type=MESH,
        )

    def right_copy(t, r):
        w = rep * here + t
        return pltpu.make_async_remote_copy(
            right.at[0, t, r], rbuf.at[w], r_send, r_recv.at[w],
            device_id=(behind, sec, r), device_id_type=MESH,
        )

    for i in range(2):
        @pl.loop(0, here)
        def _(t):
            left_copy(t, (sec + i) % 2).start()
            right_copy(t, (sec + i) % 2).start()

    def start_halo(k):
        for n, d in enumerate(shifts):
            pltpu.make_async_remote_copy(
                slots[k].at[HALO], slots[k].at[HALO - d],
                halo_send.at[k, n], halo_recv.at[k, n],
                device_id=at_sector(d), device_id_type=MESH,
            ).start()

    def wait_halo(k):
        for n, d in enumerate(shifts):
            pltpu.make_async_remote_copy(
                slots[k].at[HALO], slots[k].at[HALO - d],
                halo_send.at[k, n], halo_recv.at[k, n],
                device_id=at_sector(d), device_id_type=MESH,
            ).wait_recv()

    def exchange_start(buf, k, mine, peers, send, recv):
        for p in peers:
            pltpu.make_async_remote_copy(
                buf.at[k, mine], buf.at[k, mine], send.at[k], recv.at[k],
                device_id=p, device_id_type=MESH,
            ).start()

    def exchange_wait(buf, k, n, sem):
        some = buf.at[k, pl.ds(0, n)]
        pltpu.make_async_copy(some, some, sem.at[k]).wait()

    def total_of(buf, k, n):
        total = buf[k, 0]
        for i in range(1, n):
            total = total + buf[k, i]
        return total

    lanes = lax.broadcasted_iota(jnp.int32, (SUMS, 128), 1)
    diagonal = lanes == lax.broadcasted_iota(jnp.int32, (SUMS, 128), 0)

    def reduce_first(k, rows):
        rows = rows + [jnp.zeros((SUMS - len(rows), 128), F32)]
        sums = jnp.sum(jnp.concatenate(rows, axis=0), axis=1, keepdims=True)
        red_y[k, mine_y] = jnp.sum(jnp.where(diagonal, sums, 0.0), axis=0, keepdims=True)
        exchange_start(red_y, k, mine_y, y_peers, y_send, y_recv)

    def reduce_second(k):
        exchange_wait(red_y, k, 2 * NY - 1, y_recv)
        red_z[k, z] = total_of(red_y, k, 2 * NY)
        exchange_start(red_z, k, z, z_peers, z_send, z_recv)

    def reduce_last(k):
        exchange_wait(red_z, k, nz - 1, z_recv)
        total = jnp.where(diagonal, total_of(red_z, k, nz), 0.0)
        return jnp.sum(total, axis=1, keepdims=True) * (1.0 / count)

    near = [at_yz(0, d, rep) for d in (-1, 1)] + [at_yz(d, 0, rep) for d in (-1, 1)]
    for p in near:
        pl.semaphore_signal(near_sem, inc=1, device_id=p, device_id_type=MESH)
    pl.semaphore_wait(near_sem, len(near))
    far = [at_yz(0, d, rep) for d in (-2, 2)]
    for p in far:
        pl.semaphore_signal(far_sem, inc=1, device_id=p, device_id_type=MESH)
    pl.semaphore_wait(far_sem, len(far))

    pat_copy = pltpu.make_async_remote_copy(
        pattern.at[0], pat_v, pat_send, pat_recv, device_id=(seg, sec, other), device_id_type=MESH
    )
    pat_copy.start()
    for c in loads:
        c.wait()

    rows = lax.broadcasted_iota(jnp.int32, (size, size), 0)
    cols = lax.broadcasted_iota(jnp.int32, (size, size), 1)
    inside = (rows < kl_s[0, rep]) & (cols < kr_s[0, rep])
    mask[...] = inside.astype(F32)
    start = mask[...] * psi_v[...]
    v0[...] = start
    reduce_first(INITIAL, [column_sums(start * start)])

    pat_copy.wait_recv()
    move = pltpu.make_async_copy(pat_v, pat_s.at[other], load.at[0])
    move.start()
    move.wait()

    for k in range(ITERS):
        slots[k][2 * HALO + 1] = jnp.zeros((size, size), BF16)

    @pl.loop(0, terms)
    def _(w):
        c = charge_s[w]
        to = sector + c
        index[w] = jnp.where((to >= 0) & (to < sectors), c + HALO, 2 * HALO + 1)

    reduce_second(INITIAL)
    scale = reduce_last(INITIAL)[0:1]
    v0[...] = v0[...] * lax.rsqrt(scale + 1e-06)
    slots[0][HALO] = v0[...].astype(BF16)
    start_halo(0)

    def apply_local(k):
        half = size // 2

        @pl.loop(0, 2)
        def _(i):
            some = pl.ds(pl.multiple_of(i * half, half), half)
            first = jnp.dot(blk_v[some, :], slots[k][HALO], preferred_element_type=F32)
            acc[some, :] = first + nt_dot(slots[k][HALO, some, :], blk_v[...])

    def term(k, q, t):
        w = q * here + t
        moved = slots[k][index[w]]
        inner = jnp.dot(lbuf[w], moved, preferred_element_type=F32)
        inner = (inner * pat_s[q, rep, t].astype(F32)).astype(BF16)
        return nt_dot(inner, rbuf[w])

    def env_wait(w):
        pltpu.make_async_remote_copy(
            left.at[0, 0, 0], lbuf.at[w], l_send, l_recv.at[w],
            device_id=(ahead, sec, rep), device_id_type=MESH,
        ).wait_recv()
        pltpu.make_async_remote_copy(
            right.at[0, 0, 0], rbuf.at[w], r_send, r_recv.at[w],
            device_id=(behind, sec, rep), device_id_type=MESH,
        ).wait_recv()

    def apply_rest(k):
        wait_halo(k)
        total = acc[...]
        for t in range(here):
            for q in range(2):
                total = total + term(k, q, t)
        return total

    def offer(k, x):
        slots[k][HALO] = x.astype(BF16)
        start_halo(k)

    def dot(a, b):
        return column_sums(a * b)

    def coefficients(means, vu, vw, vv, ww):
        alpha = means[vu : vu + 1]
        rest = means[ww : ww + 1] - 2.0 * alpha * means[vw : vw + 1] + alpha * alpha * means[vv : vv + 1]
        return alpha, jnp.sqrt(jnp.maximum(rest, 0.0) + 1e-06)

    def following(alpha, square, vu, vw, vv, ww, wu, uu, wh, vh, hh, uh):
        inverse = 1.0 / square
        alpha_next = (wh - alpha * (wu + vh) + alpha * alpha * vu) * inverse
        ww_next = (
            hh + alpha * alpha * uu + square * square * vv
            - 2.0 * (alpha * uh + square * vh) + 2.0 * alpha * square * vu
        ) * inverse
        vv_next = (ww - 2.0 * alpha * vw + alpha * alpha * vv) * inverse
        vw_next = alpha_next - vw + alpha * vv
        rest = ww_next - 2.0 * alpha_next * vw_next + alpha_next * alpha_next * vv_next
        return alpha_next, jnp.sqrt(jnp.maximum(rest, 0.0) + 1e-06)

    apply_local(0)
    wait_halo(0)

    @pl.loop(0, here)
    def _(t):
        env_wait(t)
        env_wait(here + t)
        acc[...] += term(0, 0, t) + term(0, 1, t)

    offer(1, mask[...] * acc[...])
    e1[...] = mask[...] * acc[...]
    reduce_first(0, [dot(v0[...], e1[...]), dot(e1[...], e1[...]), dot(v0[...], v0[...])])
    apply_local(1)
    total = apply_rest(1)

    offer(2, mask[...] * total)
    e2[...] = mask[...] * total
    reduce_second(0)
    reduce_first(1, [dot(e1[...], e2[...]), dot(v0[...], e2[...]), dot(e2[...], e2[...])])
    apply_local(2)
    total = apply_rest(2)
    means0 = reduce_last(0)
    alpha0, beta0 = coefficients(means0, 0, 0, 2, 1)
    inverse0 = 1.0 / beta0

    image = (mask[...] * total - alpha0 * e2[...]) * inverse0
    offer(3, image - beta0 * e1[...])
    hu1[...] = image
    hw1[...] = image - beta0 * e1[...]
    reduce_second(1)
    apply_local(3)
    v1[...] = (e1[...] - alpha0 * v0[...]) * inverse0
    u1[...] = (e2[...] - alpha0 * e1[...]) * inverse0
    w1[...] = u1[...] - beta0 * v0[...]
    means1 = reduce_last(1)
    vu0, uu0, vv0 = (means0[i : i + 1] for i in range(3))
    uh0, vh0, hh0 = (means1[i : i + 1] for i in range(3))
    alpha1, beta1 = following(alpha0, beta0 * beta0, vu0, vu0, vv0, uu0, uu0, uu0, uh0, vh0, hh0, uh0)
    inverse1 = 1.0 / beta1
    mine[0] = (w1[...] - alpha1 * v1[...]) * inverse1
    mine[1] = (hw1[...] - alpha1 * u1[...]) * inverse1
    mine[2] = mine[1] - beta1 * v1[...]

    def final_copy(i):
        return pltpu.make_async_remote_copy(
            mine.at[i], theirs.at[i], fin_send.at[i], fin_recv.at[i],
            device_id=(seg, sec, other), device_id_type=MESH,
        )

    hu1[...] = alpha1 * hu1[...] + beta1 * beta1 * u1[...]
    v2, u2, w2 = mine[0], mine[1], mine[2]
    early = [dot(v2, u2), dot(v2, w2), dot(v2, v2), dot(w2, w2), dot(w2, u2), dot(u2, u2)]
    total = apply_rest(3)

    mine[3] = (mask[...] * total - hu1[...]) * inverse1
    h, v2, u2, w2 = mine[3], mine[0], mine[1], mine[2]
    reduce_first(2, early + [dot(w2, h), dot(v2, h), dot(h, h), dot(u2, h)])
    for i in range(4):
        final_copy(i).start()
    reduce_second(2)
    pltpu.make_async_copy(left, left, l_send).wait()
    pltpu.make_async_copy(right, right, r_send).wait()
    pat_copy.wait_send()
    for k in range(ITERS):
        for n, d in enumerate(shifts):
            pltpu.make_async_remote_copy(
                slots[k].at[HALO], slots[k].at[HALO - d],
                halo_send.at[k, n], halo_recv.at[k, n],
                device_id=at_sector(d), device_id_type=MESH,
            ).wait_send()
    for k in (0, 1, INITIAL):
        exchange_wait(red_z, k, nz - 1, z_send)
        exchange_wait(red_y, k, 2 * NY - 1, y_send)
    for i in range(4):
        final_copy(i).wait()
    means = reduce_last(2)
    vu, vw, vv, ww, wu, uu, wh, vh, hh, uh = (means[i : i + 1] for i in range(10))
    alpha2, beta2 = coefficients(means, 0, 1, 2, 3)
    square2 = beta2 * beta2
    alpha3, beta3 = following(alpha2, square2, vu, vw, vv, ww, wu, uu, wh, vh, hh, uh)
    coeffs[...] = jnp.concatenate([alpha0, alpha1, alpha2, alpha3, beta0, beta1, beta2, beta3], axis=1)
    outer = 1.0 / (beta2 * beta3)
    along_v = (alpha3 * alpha2 - square2) * outer
    along_u, along_w = -alpha2 * outer, -alpha3 * outer

    def last_vector(parts):
        return outer * parts[3] + along_u * parts[1] + along_w * parts[2] + along_v * parts[0]

    out[0, rep] = last_vector(mine)
    out[0, other] = last_vector(theirs)

    exchange_wait(red_z, 2, nz - 1, z_send)
    exchange_wait(red_y, 2, 2 * NY - 1, y_send)


def on_device(nseg, nsec, psi, left, right, block, keep_l, keep_r, pattern, charge):
    here, size = left.shape[1], left.shape[3]
    count = 2 * nsec * size * size
    nz = nsec // NY
    pin = lambda x: pltpu.with_memory_space_constraint(x, pltpu.HBM)
    vmem = pl.BlockSpec(memory_space=pltpu.VMEM)
    hbm = pl.BlockSpec(memory_space=pltpu.HBM)
    square = (size, size)
    dma = pltpu.SemaphoreType.DMA
    halo = pltpu.VMEM((2 * HALO + 2, *square), BF16)
    terms = 2 * here
    return pl.pallas_call(
        functools.partial(kernel, nseg, nsec, here, size, count),
        out_shape=(
            jax.ShapeDtypeStruct(psi.shape, F32),
            jax.ShapeDtypeStruct((1, 2 * ITERS), F32),
        ),
        in_specs=[hbm] * 8,
        out_specs=(vmem, vmem),
        scratch_shapes=[
            pltpu.VMEM((terms, *square), BF16),
            pltpu.VMEM((terms, *square), BF16),
            halo, halo, halo, halo,
            pltpu.VMEM(square, F32),
            pltpu.VMEM(square, F32),
            *[pltpu.VMEM(square, F32)] * 8,
            pltpu.VMEM((4, *square), F32),
            pltpu.VMEM((4, *square), F32),
            pltpu.VMEM(square, F32),
            pltpu.VMEM(square, BF16),
            pltpu.VMEM((2, here), jnp.int32),
            pltpu.SMEM((2, 2, here), jnp.int32),
            pltpu.SMEM((1, 2), jnp.int32),
            pltpu.SMEM((1, 2), jnp.int32),
            pltpu.SMEM((terms,), jnp.int32),
            pltpu.SMEM((terms,), jnp.int32),
            pltpu.VMEM((ROUNDS, nz, 1, 128), F32),
            pltpu.VMEM((ROUNDS, 2 * NY, 1, 128), F32),
            pltpu.SemaphoreType.REGULAR, pltpu.SemaphoreType.REGULAR,
            dma((6,)), dma, dma, dma((terms,)), dma((terms,)),
            dma((ITERS, 4)), dma((ITERS, 4)),
            dma((ROUNDS,)), dma((ROUNDS,)),
            dma((ROUNDS,)), dma((ROUNDS,)),
            dma, dma, dma((4,)), dma((4,)),
        ],
        compiler_params=pltpu.CompilerParams(
            collective_id=0, has_side_effects=True, vmem_limit_bytes=48 << 20
        ),
    )(*map(pin, (psi, left, right, block, keep_l, keep_r, jnp.transpose(pattern, (0, 2, 1)), charge)))


def solution(mesh):
    placed = (
        P("seg", "sec", None, None),
        P("seg", "rep", "sec", None, None),
        P("seg", "rep", "sec", None, None),
        P("seg", "sec", None, None),
        P("seg", "sec"),
        P("seg", "sec"),
        P("seg", "rep", "sec"),
        P(),
    )
    return jax.shard_map(
        functools.partial(on_device, mesh.shape["seg"], mesh.shape["sec"]),
        mesh=mesh,
        in_specs=placed,
        out_specs=(P("seg", "sec", None, None), P("seg", None)),
        check_vma=False,
    )
```

```python
import functools

import jax
import jax.numpy as jnp
from jax import lax
from jax.experimental import pallas as pl
from jax.experimental.pallas import tpu as pltpu
from jax.sharding import PartitionSpec as P

ITERS = 4
NY = 4
HALO = 2
ROUNDS = 4
INITIAL = ROUNDS - 1
SUMS = 16
F32 = jnp.float32
BF16 = jnp.bfloat16
MESH = pl.DeviceIdType.MESH


def nt_dot(a, b):
    return lax.dot_general(a, b, (((1,), (1,)), ((), ())), preferred_element_type=F32)


def outward(n):
    return sorted(range(1, n), key=lambda i: -min(i, n - i))


def column_sums(x):
    total = jnp.sum(x, axis=0, keepdims=True)
    width = total.shape[1] // 2
    return total[:, :width] + total[:, width:]


def kernel(
    nseg, nsec, here, size, count,
    psi, left, right, block, keep_l, keep_r, pattern, charge,
    out, coeffs,
    lbuf, rbuf, vs0, vs1, vs2, vs3, acc, mask, v0, e1, e2, v1, u1, w1, hu1, hw1, mine, theirs,
    psi_v, blk_v, pat_v, pat_s, kl_s, kr_s, charge_s, index, red_z, red_y,
    near_sem, far_sem, load, l_send, r_send, l_recv, r_recv, halo_send, halo_recv,
    z_send, z_recv, y_send, y_recv, pat_send, pat_recv, fin_send, fin_recv,
):
    slots = (vs0, vs1, vs2, vs3)
    seg, sec, rep = lax.axis_index("seg"), lax.axis_index("sec"), lax.axis_index("rep")
    nz = nsec // NY
    z, y = sec // NY, sec % NY
    other = 1 - rep
    sector, sectors = 2 * sec + rep, 2 * nsec
    ahead, behind = (seg + 1) % nseg, (seg + nseg - 1) % nseg
    terms = 2 * here

    def at_sector(shift):
        s = (sector + sectors + shift) % sectors
        return (seg, s // 2, s % 2)

    sign = 2 * rep - 1
    shifts = (sign, 2 * sign, -2 * sign, -sign)
    z_peers = [(seg, ((z + i) % nz) * NY + y, rep) for i in outward(nz)]
    mine_y = 2 * y + rep
    y_peers = []
    for i in outward(2 * NY):
        p = (mine_y + i) % (2 * NY)
        y_peers.append((seg, z * NY + p // 2, p % 2))

    def at_yz(dy, dz, r):
        return (seg, ((z + nz + dz) % nz) * NY + (y + NY + dy) % NY, r)

    partners = [(a, sec, jnp.int32(r)) for a in (ahead, behind) for r in range(2)]
    partners += [at_yz(0, d, rep) for d in (-1, 1)]
    partners += [at_yz(d, 0, jnp.int32(r)) for d in (-1, 1) for r in range(2)]
    partners += [(seg, sec, other)]
    barrier = pltpu.get_barrier_semaphore()
    for p in partners:
        pl.semaphore_signal(barrier, inc=1, device_id=p, device_id_type=MESH)
    loads = [
        pltpu.make_async_copy(a, b, load.at[i])
        for i, (a, b) in enumerate([
            (psi.at[0, rep], psi_v), (block.at[0, rep], blk_v), (pattern.at[0], pat_s.at[rep]),
            (keep_l, kl_s), (keep_r, kr_s), (charge, charge_s),
        ])
    ]
    for c in loads:
        c.start()
    pl.semaphore_wait(barrier, len(partners))

    def left_copy(t, r):
        w = rep * here + t
        return pltpu.make_async_remote_copy(
            left.at[0, t, r], lbuf.at[w], l_send, l_recv.at[w],
            device_id=(ahead, sec, r), device_id_type=MESH,
        )

    def right_copy(t, r):
        w = rep * here + t
        return pltpu.make_async_remote_copy(
            right.at[0, t, r], rbuf.at[w], r_send, r_recv.at[w],
            device_id=(behind, sec, r), device_id_type=MESH,
        )

    for i in range(2):
        @pl.loop(0, here)
        def _(t):
            left_copy(t, (sec + i) % 2).start()
            right_copy(t, (sec + i) % 2).start()

    def start_halo(k):
        for n, d in enumerate(shifts):
            pltpu.make_async_remote_copy(
                slots[k].at[HALO], slots[k].at[HALO - d],
                halo_send.at[k, n], halo_recv.at[k, n],
                device_id=at_sector(d), device_id_type=MESH,
            ).start()

    def wait_halo(k):
        for n, d in enumerate(shifts):
            pltpu.make_async_remote_copy(
                slots[k].at[HALO], slots[k].at[HALO - d],
                halo_send.at[k, n], halo_recv.at[k, n],
                device_id=at_sector(d), device_id_type=MESH,
            ).wait_recv()

    def exchange_start(buf, k, mine, peers, send, recv):
        for p in peers:
            pltpu.make_async_remote_copy(
                buf.at[k, mine], buf.at[k, mine], send.at[k], recv.at[k],
                device_id=p, device_id_type=MESH,
            ).start()

    def exchange_wait(buf, k, n, sem):
        some = buf.at[k, pl.ds(0, n)]
        pltpu.make_async_copy(some, some, sem.at[k]).wait()

    def total_of(buf, k, n):
        total = buf[k, 0]
        for i in range(1, n):
            total = total + buf[k, i]
        return total

    lanes = lax.broadcasted_iota(jnp.int32, (SUMS, 128), 1)
    diagonal = lanes == lax.broadcasted_iota(jnp.int32, (SUMS, 128), 0)

    def reduce_first(k, rows):
        rows = rows + [jnp.zeros((SUMS - len(rows), 128), F32)]
        sums = jnp.sum(jnp.concatenate(rows, axis=0), axis=1, keepdims=True)
        red_y[k, mine_y] = jnp.sum(jnp.where(diagonal, sums, 0.0), axis=0, keepdims=True)
        exchange_start(red_y, k, mine_y, y_peers, y_send, y_recv)

    def reduce_second(k):
        exchange_wait(red_y, k, 2 * NY - 1, y_recv)
        red_z[k, z] = total_of(red_y, k, 2 * NY)
        exchange_start(red_z, k, z, z_peers, z_send, z_recv)

    def reduce_last(k):
        exchange_wait(red_z, k, nz - 1, z_recv)
        total = jnp.where(diagonal, total_of(red_z, k, nz), 0.0)
        return jnp.sum(total, axis=1, keepdims=True) * (1.0 / count)

    near = [at_yz(0, d, rep) for d in (-1, 1)] + [at_yz(d, 0, rep) for d in (-1, 1)]
    for p in near:
        pl.semaphore_signal(near_sem, inc=1, device_id=p, device_id_type=MESH)
    pl.semaphore_wait(near_sem, len(near))
    far = [at_yz(0, d, rep) for d in (-2, 2)]
    for p in far:
        pl.semaphore_signal(far_sem, inc=1, device_id=p, device_id_type=MESH)
    pl.semaphore_wait(far_sem, len(far))

    pat_copy = pltpu.make_async_remote_copy(
        pattern.at[0], pat_v, pat_send, pat_recv, device_id=(seg, sec, other), device_id_type=MESH
    )
    pat_copy.start()
    for c in loads:
        c.wait()

    rows = lax.broadcasted_iota(jnp.int32, (size, size), 0)
    cols = lax.broadcasted_iota(jnp.int32, (size, size), 1)
    inside = (rows < kl_s[0, rep]) & (cols < kr_s[0, rep])
    mask[...] = inside.astype(F32)
    start = mask[...] * psi_v[...]
    v0[...] = start
    reduce_first(INITIAL, [column_sums(start * start)])

    pat_copy.wait_recv()
    move = pltpu.make_async_copy(pat_v, pat_s.at[other], load.at[0])
    move.start()
    move.wait()

    for k in range(ITERS):
        slots[k][2 * HALO + 1] = jnp.zeros((size, size), BF16)

    @pl.loop(0, terms)
    def _(w):
        c = charge_s[w]
        to = sector + c
        index[w] = jnp.where((to >= 0) & (to < sectors), c + HALO, 2 * HALO + 1)

    reduce_second(INITIAL)
    scale = reduce_last(INITIAL)[0:1]
    v0[...] = v0[...] * lax.rsqrt(scale + 1e-06)
    slots[0][HALO] = v0[...].astype(BF16)
    start_halo(0)

    def apply_local(k):
        half = size // 2

        @pl.loop(0, 2)
        def _(i):
            some = pl.ds(pl.multiple_of(i * half, half), half)
            first = jnp.dot(blk_v[some, :], slots[k][HALO], preferred_element_type=F32)
            acc[some, :] = first + nt_dot(slots[k][HALO, some, :], blk_v[...])

    def term(k, q, t):
        w = q * here + t
        moved = slots[k][index[w]]
        inner = jnp.dot(lbuf[w], moved, preferred_element_type=F32)
        inner = (inner * pat_s[q, rep, t].astype(F32)).astype(BF16)
        return nt_dot(inner, rbuf[w])

    def env_wait(w):
        pltpu.make_async_remote_copy(
            left.at[0, 0, 0], lbuf.at[w], l_send, l_recv.at[w],
            device_id=(ahead, sec, rep), device_id_type=MESH,
        ).wait_recv()
        pltpu.make_async_remote_copy(
            right.at[0, 0, 0], rbuf.at[w], r_send, r_recv.at[w],
            device_id=(behind, sec, rep), device_id_type=MESH,
        ).wait_recv()

    def apply_rest(k):
        wait_halo(k)
        total = acc[...]
        for t in range(here):
            for q in range(2):
                total = total + term(k, q, t)
        return total

    def offer(k, x):
        slots[k][HALO] = x.astype(BF16)
        start_halo(k)

    def dot(a, b):
        return column_sums(a * b)

    def coefficients(means, vu, vw, vv, ww):
        alpha = means[vu : vu + 1]
        rest = means[ww : ww + 1] - 2.0 * alpha * means[vw : vw + 1] + alpha * alpha * means[vv : vv + 1]
        return alpha, jnp.sqrt(jnp.maximum(rest, 0.0) + 1e-06)

    def following(alpha, square, vu, vw, vv, ww, wu, uu, wh, vh, hh, uh):
        inverse = 1.0 / square
        alpha_next = (wh - alpha * (wu + vh) + alpha * alpha * vu) * inverse
        ww_next = (
            hh + alpha * alpha * uu + square * square * vv
            - 2.0 * (alpha * uh + square * vh) + 2.0 * alpha * square * vu
        ) * inverse
        vv_next = (ww - 2.0 * alpha * vw + alpha * alpha * vv) * inverse
        vw_next = alpha_next - vw + alpha * vv
        rest = ww_next - 2.0 * alpha_next * vw_next + alpha_next * alpha_next * vv_next
        return alpha_next, jnp.sqrt(jnp.maximum(rest, 0.0) + 1e-06)

    apply_local(0)
    wait_halo(0)

    @pl.loop(0, here)
    def _(t):
        env_wait(t)
        env_wait(here + t)
        acc[...] += term(0, 0, t) + term(0, 1, t)

    offer(1, mask[...] * acc[...])
    e1[...] = mask[...] * acc[...]
    reduce_first(0, [dot(v0[...], e1[...]), dot(e1[...], e1[...]), dot(v0[...], v0[...])])
    apply_local(1)
    total = apply_rest(1)

    offer(2, mask[...] * total)
    e2[...] = mask[...] * total
    reduce_second(0)
    reduce_first(1, [dot(e1[...], e2[...]), dot(v0[...], e2[...]), dot(e2[...], e2[...])])
    apply_local(2)
    total = apply_rest(2)
    means0 = reduce_last(0)
    alpha0, beta0 = coefficients(means0, 0, 0, 2, 1)
    inverse0 = 1.0 / beta0

    image = (mask[...] * total - alpha0 * e2[...]) * inverse0
    offer(3, image - beta0 * e1[...])
    hu1[...] = image
    hw1[...] = image - beta0 * e1[...]
    reduce_second(1)
    apply_local(3)
    v1[...] = (e1[...] - alpha0 * v0[...]) * inverse0
    u1[...] = (e2[...] - alpha0 * e1[...]) * inverse0
    w1[...] = u1[...] - beta0 * v0[...]
    means1 = reduce_last(1)
    vu0, uu0, vv0 = (means0[i : i + 1] for i in range(3))
    uh0, vh0, hh0 = (means1[i : i + 1] for i in range(3))
    alpha1, beta1 = following(alpha0, beta0 * beta0, vu0, vu0, vv0, uu0, uu0, uu0, uh0, vh0, hh0, uh0)
    inverse1 = 1.0 / beta1
    mine[0] = (w1[...] - alpha1 * v1[...]) * inverse1
    mine[1] = (hw1[...] - alpha1 * u1[...]) * inverse1
    mine[2] = mine[1] - beta1 * v1[...]

    def final_copy(i):
        return pltpu.make_async_remote_copy(
            mine.at[i], theirs.at[i], fin_send.at[i], fin_recv.at[i],
            device_id=(seg, sec, other), device_id_type=MESH,
        )

    hu1[...] = alpha1 * hu1[...] + beta1 * beta1 * u1[...]
    v2, u2, w2 = mine[0], mine[1], mine[2]
    early = [dot(v2, u2), dot(v2, w2), dot(v2, v2), dot(w2, w2), dot(w2, u2), dot(u2, u2)]
    total = apply_rest(3)

    mine[3] = (mask[...] * total - hu1[...]) * inverse1
    h, v2, u2, w2 = mine[3], mine[0], mine[1], mine[2]
    reduce_first(2, early + [dot(w2, h), dot(v2, h), dot(h, h), dot(u2, h)])
    reduce_second(2)
    for i in range(4):
        final_copy(i).start()
    pltpu.make_async_copy(left, left, l_send).wait()
    pltpu.make_async_copy(right, right, r_send).wait()
    pat_copy.wait_send()
    for k in range(ITERS):
        for n, d in enumerate(shifts):
            pltpu.make_async_remote_copy(
                slots[k].at[HALO], slots[k].at[HALO - d],
                halo_send.at[k, n], halo_recv.at[k, n],
                device_id=at_sector(d), device_id_type=MESH,
            ).wait_send()
    for k in (0, 1, INITIAL):
        exchange_wait(red_z, k, nz - 1, z_send)
        exchange_wait(red_y, k, 2 * NY - 1, y_send)
    for i in range(4):
        final_copy(i).wait()
    means = reduce_last(2)
    vu, vw, vv, ww, wu, uu, wh, vh, hh, uh = (means[i : i + 1] for i in range(10))
    alpha2, beta2 = coefficients(means, 0, 1, 2, 3)
    square2 = beta2 * beta2
    alpha3, beta3 = following(alpha2, square2, vu, vw, vv, ww, wu, uu, wh, vh, hh, uh)
    coeffs[...] = jnp.concatenate([alpha0, alpha1, alpha2, alpha3, beta0, beta1, beta2, beta3], axis=1)
    outer = 1.0 / (beta2 * beta3)
    along_v = (alpha3 * alpha2 - square2) * outer
    along_u, along_w = -alpha2 * outer, -alpha3 * outer

    def last_vector(parts):
        return outer * parts[3] + along_u * parts[1] + along_w * parts[2] + along_v * parts[0]

    out[0, rep] = last_vector(mine)
    out[0, other] = last_vector(theirs)

    exchange_wait(red_z, 2, nz - 1, z_send)
    exchange_wait(red_y, 2, 2 * NY - 1, y_send)


def on_device(nseg, nsec, psi, left, right, block, keep_l, keep_r, pattern, charge):
    here, size = left.shape[1], left.shape[3]
    count = 2 * nsec * size * size
    nz = nsec // NY
    pin = lambda x: pltpu.with_memory_space_constraint(x, pltpu.HBM)
    vmem = pl.BlockSpec(memory_space=pltpu.VMEM)
    hbm = pl.BlockSpec(memory_space=pltpu.HBM)
    square = (size, size)
    dma = pltpu.SemaphoreType.DMA
    halo = pltpu.VMEM((2 * HALO + 2, *square), BF16)
    terms = 2 * here
    return pl.pallas_call(
        functools.partial(kernel, nseg, nsec, here, size, count),
        out_shape=(
            jax.ShapeDtypeStruct(psi.shape, F32),
            jax.ShapeDtypeStruct((1, 2 * ITERS), F32),
        ),
        in_specs=[hbm] * 8,
        out_specs=(vmem, vmem),
        scratch_shapes=[
            pltpu.VMEM((terms, *square), BF16),
            pltpu.VMEM((terms, *square), BF16),
            halo, halo, halo, halo,
            pltpu.VMEM(square, F32),
            pltpu.VMEM(square, F32),
            *[pltpu.VMEM(square, F32)] * 8,
            pltpu.VMEM((4, *square), F32),
            pltpu.VMEM((4, *square), F32),
            pltpu.VMEM(square, F32),
            pltpu.VMEM(square, BF16),
            pltpu.VMEM((2, here), jnp.int32),
            pltpu.SMEM((2, 2, here), jnp.int32),
            pltpu.SMEM((1, 2), jnp.int32),
            pltpu.SMEM((1, 2), jnp.int32),
            pltpu.SMEM((terms,), jnp.int32),
            pltpu.SMEM((terms,), jnp.int32),
            pltpu.VMEM((ROUNDS, nz, 1, 128), F32),
            pltpu.VMEM((ROUNDS, 2 * NY, 1, 128), F32),
            pltpu.SemaphoreType.REGULAR, pltpu.SemaphoreType.REGULAR,
            dma((6,)), dma, dma, dma((terms,)), dma((terms,)),
            dma((ITERS, 4)), dma((ITERS, 4)),
            dma((ROUNDS,)), dma((ROUNDS,)),
            dma((ROUNDS,)), dma((ROUNDS,)),
            dma, dma, dma((4,)), dma((4,)),
        ],
        compiler_params=pltpu.CompilerParams(
            collective_id=0, has_side_effects=True, vmem_limit_bytes=48 << 20
        ),
    )(*map(pin, (psi, left, right, block, keep_l, keep_r, jnp.transpose(pattern, (0, 2, 1)), charge)))


def solution(mesh):
    placed = (
        P("seg", "sec", None, None),
        P("seg", "rep", "sec", None, None),
        P("seg", "rep", "sec", None, None),
        P("seg", "sec", None, None),
        P("seg", "sec"),
        P("seg", "sec"),
        P("seg", "rep", "sec"),
        P(),
    )
    return jax.shard_map(
        functools.partial(on_device, mesh.shape["seg"], mesh.shape["sec"]),
        mesh=mesh,
        in_specs=placed,
        out_specs=(P("seg", "sec", None, None), P("seg", None)),
        check_vma=False,
    )
```
